32 devices in a mesh: fsdp: 4 (over z), ctx: 2 (over x), tp: 4 (over y, core).
Axes of the slice: x: 2, y: 2, z: 4, core: 2. Of those that a mesh axis runs over, the one named last changes fastest.
Arguments:
- tokens: bfloat16 [6144, 1600], P(('fsdp', 'ctx')), may hold values from -6 to 6
- segments: int32 [6144], P('fsdp'), may hold values from 0 to 15, never falling along the last dimension, each value on 1 to 768 neighbouring positions
- first_gain: bfloat16 [1600], P('fsdp'), may hold values from 0.5 to 1.5
- first_bias: bfloat16 [1600], P('fsdp'), may hold values from -1.5 to 1.5
- input_weight: bfloat16 [1600, 4800], P('fsdp'), may hold values from -2 to 2
- query_bias: bfloat16 [1600], P('fsdp'), may hold values from -1.5 to 1.5
- value_bias: bfloat16 [1600], P('fsdp'), may hold values from -1.5 to 1.5
- output_weight: bfloat16 [1600, 1600], P('fsdp'), may hold values from -0.625 to 0.625
- output_bias: bfloat16 [1600], P('fsdp'), may hold values from -1.5 to 1.5
- second_gain: bfloat16 [1600], P('fsdp'), may hold values from 0.5 to 1.5
- second_bias: bfloat16 [1600], P('fsdp'), may hold values from -1.5 to 1.5
- up_weight: bfloat16 [1600, 6400], P('fsdp', 'tp'), may hold values from -0.15625 to 0.15625
- up_bias: bfloat16 [6400], P(('tp', 'fsdp')), may hold values from -1.5 to 1.5
- down_weight: bfloat16 [6400, 1600], P('tp', 'fsdp'), may hold values from -0.078125 to 0.078125
- down_bias: bfloat16 [1600], P('fsdp'), may hold values from -1.5 to 1.5
- cotangent: bfloat16 [6144, 1600], P(('fsdp', 'ctx')), may hold values from -6 to 6
Outputs:
- result: bfloat16 [6144, 1600], P(('fsdp', 'ctx'))
- token_gradient: bfloat16 [6144, 1600], P(('fsdp', 'ctx'))
- first_gain_gradient: float32 [1600], P('fsdp')
- first_bias_gradient: float32 [1600], P('fsdp')
- input_weight_gradient: float32 [1600, 4800], P('fsdp')
- query_bias_gradient: float32 [1600], P('fsdp')
- value_bias_gradient: float32 [1600], P('fsdp')
- output_weight_gradient: float32 [1600, 1600], P('fsdp')
- output_bias_gradient: float32 [1600], P('fsdp')
- second_gain_gradient: float32 [1600], P('fsdp')
- second_bias_gradient: float32 [1600], P('fsdp')
- up_weight_gradient: float32 [1600, 6400], P('fsdp', 'tp')
- up_bias_gradient: float32 [6400], P(('tp', 'fsdp'))
- down_weight_gradient: float32 [6400, 1600], P('tp', 'fsdp')
- down_bias_gradient: float32 [1600], P('fsdp')
The draws below stay inside these ranges and needn't reach their ends.
Inputs may be any that keep to these rules, and one draw needn't show every extreme that they name: `segments`: segment numbers never fall along the tokens; each segment holds 1 to 768 tokens, one exactly 768.
All inputs are finite; a program needn't handle non-finite values.
Results may differ from the reference program's by a relative error of at most 0.012.
Values may be sent and summed in bfloat16 or wider, within the bound.
No kernel may reach another device: no remote copies, remote signals or barrier semaphores. Data moves between devices by JAX's collectives and lax.ppermute only.
A program may use at most 256 MiB of HBM per device.

```python
import math
import jax
import jax.numpy as jnp
import numpy as np
from jax import lax

D = 1600
HEADS = 25
HEAD = 64
FF = 6400
ROWS = 768
TOKENS = 6144
DOCS = 16
N_FSDP = 4
N_CTX = 2


def draw_input_weight(key, part):
    return (jax.random.normal(key, (D, 3 * D), jnp.float32) * (1.0 / D) ** 0.5).astype(jnp.bfloat16)


def steps_of(stream_key, shape, cuts, low, largest):
    def one(dim, blocks):
        heights = jax.random.uniform(jax.random.fold_in(jax.random.fold_in(stream_key, 6), dim), (blocks,), jnp.float32, low / len(cuts), largest / len(cuts))
        return jnp.repeat(jnp.exp(heights), shape[dim] // blocks).reshape((-1,) + (1,) * (len(shape) - dim - 1))

    level = one(*cuts[0])
    for cut in cuts[1:]:
        level = level * one(*cut)
    return level


def length_profile(number_of, total, most, slope):
    portions = [(1 << 20) // math.isqrt(standing ** slope) + 1 for standing in range(2, number_of + 1)]
    spare, given = total - most - (number_of - 1), [1] * (number_of - 1)
    while spare > 0:
        free = [i for i in range(number_of - 1) if given[i] < most]
        whole, left = sum([portions[i] for i in free]), spare
        for i in free:
            more = min(most - given[i], max(1, left * portions[i] // whole), spare)
            given[i] = given[i] + more
            spare = spare - more
    return np.array([most] + given)


def ragged(own_key, count, total, most, lean):
    if count == 2:
        one = jax.random.randint(own_key, (), max(1, total - most), min(most, total - 1) + 1)
        return jnp.stack([one, total - one])
    sizes = jnp.asarray(length_profile(count, total, most, lean), jnp.int32)
    pairs = (count - 1) // 2
    donor, taker = sizes[1:1 + 2 * pairs:2], sizes[2:2 + 2 * pairs:2]
    room = jnp.minimum(donor - 1, most - taker)
    moved = jax.random.randint(jax.random.fold_in(own_key, 1), (pairs,), 0, 1 << 20) % (room + 1)
    sizes = sizes.at[1:1 + 2 * pairs:2].set(donor - moved).at[2:2 + 2 * pairs:2].set(taker + moved)
    return sizes[jax.random.permutation(jax.random.fold_in(own_key, 2), count)]


def gaussian(stream_key, extent, width, bound, split=(), kind=jnp.bfloat16):
    result = width * jax.random.normal(stream_key, extent, jnp.float32)
    if split:
        result = result * steps_of(stream_key, extent, split, -0.22, 0.18)
    return jnp.clip(result, -bound, bound).astype(kind)


def setup_inputs(seed: int = 0) -> dict:
    key_list = jax.random.split(jax.random.key(seed), 17)
    return {
        "tokens": gaussian(key_list[0], (TOKENS, D), 1.0, 6.0, ((0, 8),)),
        "segments": jnp.searchsorted(jnp.cumsum(ragged(key_list[1], DOCS, TOKENS, ROWS, 1)), jnp.arange(TOKENS), side="right").astype(jnp.int32),
        "first_gain": jnp.clip(1.0 + 0.1 * jax.random.normal(key_list[2], (D,), jnp.float32), 0.5, 1.5).astype(jnp.bfloat16),
        "first_bias": gaussian(key_list[3], (D,), 0.3, 1.5, ((0, 4),)),
        "input_weight": draw_input_weight(jax.random.fold_in(key_list[16], 71), 0),
        "query_bias": gaussian(key_list[5], (D,), 0.3, 1.5, ((0, 4),)),
        "value_bias": gaussian(key_list[6], (D,), 0.3, 1.5, ((0, 4),)),
        "output_weight": gaussian(key_list[7], (D, D), (D // 16) ** -0.5, 0.625, ((0, 4),)),
        "output_bias": gaussian(key_list[8], (D,), 0.3, 1.5, ((0, 4),)),
        "second_gain": jnp.clip(1.0 + 0.1 * jax.random.normal(key_list[9], (D,), jnp.float32), 0.5, 1.5).astype(jnp.bfloat16),
        "second_bias": gaussian(key_list[10], (D,), 0.3, 1.5, ((0, 4),)),
        "up_weight": gaussian(key_list[11], (D, FF), D ** -0.5, 0.15625, ((0, 4), (1, 4))),
        "up_bias": gaussian(key_list[12], (FF,), 0.3, 1.5, ((0, 16),)),
        "down_weight": gaussian(key_list[13], (FF, D), FF ** -0.5, 0.078125, ((0, 4), (1, 4))),
        "down_bias": gaussian(key_list[14], (D,), 0.3, 1.5, ((0, 4),)),
        "cotangent": gaussian(key_list[15], (TOKENS, D), 1.0, 6.0, ((0, 8),)),
    }


EPS = 1e-05
NEGATIVE = -1e+30
HIGHEST = lax.Precision.HIGHEST

@jax.custom_vjp
def low(v):
    return lax.optimization_barrier(v.astype(jnp.bfloat16)).astype(jnp.float32)

@jax.custom_vjp
def low_back(v):
    return v

def low_keep(v):
    return (low(v), None)

def low_pass(kept, grad):
    return (grad,)

def back_keep(v):
    return (v, None)

def back_low(kept, grad):
    return (low(grad),)
low.defvjp(low_keep, low_pass)
low_back.defvjp(back_keep, back_low)

def matmul(left, right):
    return jnp.dot(left, right, precision=HIGHEST)

def layer_norm(values, gain, offset):
    centre = values - lax.optimization_barrier(jnp.mean(values, -1, keepdims=True))
    spread = lax.optimization_barrier(jnp.mean(centre * centre, -1, keepdims=True))
    return centre * lax.rsqrt(spread + EPS) * gain + offset

def residual_block(params, tokens, segments):
    gain_one, offset_one, weight_in, bias_query, bias_value, weight_out, bias_out, gain_two, offset_two, weight_up, bias_up, weight_down, bias_down = params
    length = ROWS * N_CTX
    factor = HEAD ** (-0.5)

    def to_heads(values):
        return values.reshape(length, HEADS, HEAD).transpose(1, 0, 2)

    def sequence(item_pair):
        inputs, labels = item_pair
        normed = low(layer_norm(inputs, gain_one, offset_one))
        joined = matmul(normed, weight_in)
        queries = low(low_back(joined[:, :D] + bias_query))
        keys_all = low(low_back(joined[:, D:2 * D]))
        values = low(low_back(joined[:, 2 * D:] + bias_value))
        places = jnp.arange(length)
        allowed = (labels[:, None] == labels[None, :]) & (places[None, :] <= places[:, None])

        def one_head(triple):
            head_query, head_key, head_value = triple
            scores = jnp.where(allowed, matmul(head_query, head_key.T) * factor, NEGATIVE)
            weights = low(jax.nn.softmax(low_back(scores), axis=-1))
            return matmul(weights, head_value)
        mixture = lax.map(jax.checkpoint(one_head), (to_heads(queries), to_heads(keys_all), to_heads(values)))
        mixture = low(low_back(mixture.transpose(1, 0, 2).reshape(length, D)))
        middle = inputs + low_back(matmul(mixture, weight_out) + bias_out)
        hidden_in = low(layer_norm(middle, gain_two, offset_two))
        preact = low_back(matmul(hidden_in, weight_up) + bias_up)
        activated = low(jax.nn.gelu(preact, approximate=True))
        return middle + matmul(activated, weight_down) + bias_down
    output = lax.map(jax.checkpoint(sequence), (tokens.reshape(N_FSDP, length, D), segments.reshape(N_FSDP, length)))
    return output.reshape(N_FSDP * length, D)

def reference(tokens, segments, first_gain, first_bias, input_weight, query_bias, value_bias, output_weight, output_bias, second_gain, second_bias, up_weight, up_bias, down_weight, down_bias, cotangent):
    params = (first_gain.astype(jnp.float32), first_bias.astype(jnp.float32), input_weight.astype(jnp.float32), query_bias.astype(jnp.float32), value_bias.astype(jnp.float32), output_weight.astype(jnp.float32), output_bias.astype(jnp.float32), second_gain.astype(jnp.float32), second_bias.astype(jnp.float32), up_weight.astype(jnp.float32), up_bias.astype(jnp.float32), down_weight.astype(jnp.float32), down_bias.astype(jnp.float32))
    inputs = tokens.astype(jnp.float32)

    def apply_block(weights, activations):
        return residual_block(weights, activations, segments)
    output, pullback = jax.vjp(apply_block, params, inputs)
    weight_grads, input_grads = pullback(cotangent.astype(jnp.float32))
    grad_gain_one, grad_bias_one, grad_in, grad_bias_query, grad_bias_value, grad_out, grad_bias_out, grad_gain_two, grad_bias_two, grad_up, grad_bias_up, grad_down, grad_bias_down = weight_grads
    return (output.astype(jnp.bfloat16), input_grads.astype(jnp.bfloat16), grad_gain_one, grad_bias_one, grad_in, grad_bias_query, grad_bias_value, grad_out, grad_bias_out, grad_gain_two, grad_bias_two, grad_up, grad_bias_up, grad_down, grad_bias_down)
```

```python
from functools import partial

import jax
import jax.numpy as jnp
from jax import lax
from jax.experimental import pallas as pl
from jax.experimental.layout import Layout, with_layout_constraint
from jax.experimental.pallas import tpu as pltpu
from jax.sharding import PartitionSpec as P


HEADS = 25
HEAD = 64
PAIR = 2 * HEAD
BLOCK = 256

EPS = 1e-05
NEGATIVE = -1e30
SCALE = HEAD ** (-0.5)

bf16 = jnp.bfloat16
f32 = jnp.float32


def norm_forward(values, gain, offset):
    centre = values - jnp.mean(values, -1, keepdims=True)
    inverse = lax.rsqrt(jnp.mean(centre * centre, -1, keepdims=True) + EPS)
    unit = centre * inverse
    return (unit * gain + offset, unit, inverse)


def norm_backward(upstream, unit, inverse, gain):
    scaled = upstream * gain
    inner = (
        scaled
        - jnp.mean(scaled, -1, keepdims=True)
        - unit * jnp.mean(scaled * unit, -1, keepdims=True)
    )
    return (inner * inverse, jnp.sum(upstream * unit, 0), jnp.sum(upstream, 0))


def gelu_tanh(values):
    return jax.nn.gelu(values, approximate=True)


def dot_rows(left, right):
    return lax.dot_general(left, right, (((0,), (0,)), ((), ())), preferred_element_type=f32)


def dot_lanes(left, right):
    return lax.dot_general(left, right, (((1,), (1,)), ((), ())), preferred_element_type=f32)


def dot(left, right):
    return jnp.dot(left, right, preferred_element_type=f32)


def lane_mask(which):
    lanes = lax.broadcasted_iota(jnp.int32, (1, PAIR), 1)
    return (lanes // HEAD == which).astype(f32)


def masked_pair(block, scale):
    wide = block.astype(f32)
    return [(wide * (lane_mask(h) * scale)).astype(bf16) for h in range(2)]


def allowed_block(key_block, query_block, rows, start):
    keys = key_block * BLOCK + lax.broadcasted_iota(jnp.int32, (BLOCK, BLOCK), 0)
    places = (
        rows + query_block * BLOCK + lax.broadcasted_iota(jnp.int32, (BLOCK, BLOCK), 1)
    )
    return (keys >= start) & (keys <= places)


def forward_kernel(
    low_ref, live_ref, start_ref, q_ref, k_ref, v_ref, o_ref, ot_ref, log_ref, vtbuf
):
    rows = q_ref.shape[0]
    pair = pl.program_id(0)
    live = (pair < pl.num_programs(0) - 1) | (live_ref[0] > 0)

    @pl.when(jnp.logical_not(live))
    def _():
        o_ref[...] = jnp.zeros_like(o_ref)
        ot_ref[...] = jnp.zeros_like(ot_ref)
        log_ref[...] = jnp.zeros_like(log_ref)

    @pl.when(live)
    def _():
        vtbuf[...] = v_ref[...].astype(f32).T.astype(bf16)
        for qb in range(rows // BLOCK):
            span = slice(qb * BLOCK, (qb + 1) * BLOCK)
            queries = masked_pair(q_ref[span, :], SCALE)
            start = start_ref[:, span]

            def step(kb, carry):
                base = pl.multiple_of(kb * BLOCK, BLOCK)
                keys = k_ref[pl.ds(base, BLOCK), :]
                allowed = allowed_block(kb, qb, rows, start)
                out = []
                for h in range(2):
                    highest, summed, total = carry[3 * h : 3 * h + 3]
                    scores = jnp.where(allowed, dot_lanes(keys, queries[h]), NEGATIVE)
                    higher = jnp.maximum(highest, jnp.max(scores, 0, keepdims=True))
                    fade = jnp.exp(highest - higher)
                    expo = jnp.exp(scores - higher)
                    summed = summed * fade + jnp.sum(expo, 0, keepdims=True)
                    values = vtbuf[h * HEAD : (h + 1) * HEAD, pl.ds(base, BLOCK)]
                    total = total * fade + dot(values, expo.astype(bf16))
                    out += [higher, summed, total]
                return tuple(out)

            empty = (
                jnp.full((1, BLOCK), NEGATIVE, f32),
                jnp.zeros((1, BLOCK), f32),
                jnp.zeros((HEAD, BLOCK), f32),
            )
            done = lax.fori_loop(low_ref[qb], rows // BLOCK + qb + 1, step, empty + empty)
            for h in range(2):
                highest, summed, total = done[3 * h : 3 * h + 3]
                ot_ref[h * HEAD : (h + 1) * HEAD, span] = total / summed
                log_ref[0, h : h + 1, span] = highest + jnp.log(summed)
            o_ref[span, :] = ot_ref[:, span].T.astype(bf16)


def backward_kernel(
    low_ref,
    live_ref,
    start_ref,
    q_ref,
    k_ref,
    v_ref,
    g_ref,
    ot_ref,
    log_ref,
    dq_ref,
    dk_ref,
    dv_ref,
    ktbuf,
    dkbuf,
    dvbuf,
):
    rows = q_ref.shape[0]
    pair = pl.program_id(0)
    live = (pair < pl.num_programs(0) - 1) | (live_ref[0] > 0)
    dkbuf[...] = jnp.zeros_like(dkbuf)
    dvbuf[...] = jnp.zeros_like(dvbuf)

    @pl.when(jnp.logical_not(live))
    def _():
        dq_ref[...] = jnp.zeros_like(dq_ref)

    @pl.when(live)
    def _():
        ktbuf[...] = k_ref[...].astype(f32).T.astype(bf16)
        for qb in range(rows // BLOCK):
            span = slice(qb * BLOCK, (qb + 1) * BLOCK)
            queries = masked_pair(q_ref[span, :], SCALE)
            grads = masked_pair(g_ref[span, :], 1.0)
            start = start_ref[:, span]
            turned = g_ref[span, :].astype(f32).T * ot_ref[:, span]
            inner = [jnp.sum(turned[h * HEAD : (h + 1) * HEAD], 0, keepdims=True) for h in range(2)]
            log_total = [log_ref[0, h : h + 1, span] for h in range(2)]

            def step(kb, carry):
                base = pl.multiple_of(kb * BLOCK, BLOCK)
                here = pl.ds(base, BLOCK)
                keys, values = k_ref[here, :], v_ref[here, :]
                allowed = allowed_block(kb, qb, rows, start)
                out = []
                grad_keys, grad_values = dkbuf[here, :], dvbuf[here, :]
                for h in range(2):
                    scores = jnp.where(allowed, dot_lanes(keys, queries[h]), NEGATIVE)
                    probs = jnp.exp(scores - log_total[h])
                    grad_probs = dot_lanes(values, grads[h])
                    grad_scores = (probs * (grad_probs - inner[h])).astype(bf16)
                    grad_values += dot(probs.astype(bf16), grads[h])
                    grad_keys += dot(grad_scores, queries[h])
                    turned_keys = ktbuf[h * HEAD : (h + 1) * HEAD, here]
                    out.append(carry[h] + dot(turned_keys, grad_scores))
                dkbuf[here, :] = grad_keys
                dvbuf[here, :] = grad_values
                return tuple(out)

            empty = jnp.zeros((HEAD, BLOCK), f32)
            done = lax.fori_loop(low_ref[qb], rows // BLOCK + qb + 1, step, (empty, empty))
            dq_ref[span, :] = (jnp.concatenate(done, 0) * SCALE).T.astype(bf16)

    dk_ref[...] = dkbuf[...].astype(bf16)
    dv_ref[...] = dvbuf[...].astype(bf16)


def column_spec(rows):
    return pl.BlockSpec((rows, PAIR), lambda p: (0, p))


def attention_forward(low, live, start, queries, keys, values):
    rows, width = queries.shape
    pairs = width // PAIR
    smem = pl.BlockSpec(memory_space=pltpu.SMEM)
    return pl.pallas_call(
        forward_kernel,
        grid=(pairs,),
        in_specs=[
            smem,
            smem,
            pl.BlockSpec((1, rows), lambda p: (0, 0)),
            column_spec(rows),
            column_spec(2 * rows),
            column_spec(2 * rows),
        ],
        out_specs=[
            column_spec(rows),
            pl.BlockSpec((PAIR, rows), lambda p: (p, 0)),
            pl.BlockSpec((1, 2, rows), lambda p: (p, 0, 0)),
        ],
        out_shape=[
            jax.ShapeDtypeStruct((rows, pairs * PAIR), bf16),
            jax.ShapeDtypeStruct((pairs * PAIR, rows), f32),
            jax.ShapeDtypeStruct((pairs, 2, rows), f32),
        ],
        scratch_shapes=[pltpu.VMEM((PAIR, 2 * rows), bf16)],
        cost_estimate=pl.CostEstimate(
            flops=2 * 2 * rows * rows * pairs * PAIR,
            bytes_accessed=rows * pairs * PAIR * 16,
            transcendentals=rows * rows * pairs * 2,
        ),
        name="attention_forward",
    )(low, live, start, queries, keys, values)


def attention_backward(low, live, start, queries, keys, values, grad, turned, log_total):
    rows, width = queries.shape
    pairs = width // PAIR
    smem = pl.BlockSpec(memory_space=pltpu.SMEM)
    return pl.pallas_call(
        backward_kernel,
        grid=(pairs,),
        in_specs=[
            smem,
            smem,
            pl.BlockSpec((1, rows), lambda p: (0, 0)),
            column_spec(rows),
            column_spec(2 * rows),
            column_spec(2 * rows),
            column_spec(rows),
            pl.BlockSpec((PAIR, rows), lambda p: (p, 0)),
            pl.BlockSpec((1, 2, rows), lambda p: (p, 0, 0)),
        ],
        out_specs=[column_spec(rows)] + [column_spec(2 * rows)] * 2,
        out_shape=[jax.ShapeDtypeStruct((count, pairs * PAIR), bf16) for count in (rows, 2 * rows, 2 * rows)],
        scratch_shapes=[
            pltpu.VMEM((PAIR, 2 * rows), bf16),
            pltpu.VMEM((2 * rows, PAIR), f32),
            pltpu.VMEM((2 * rows, PAIR), f32),
        ],
        cost_estimate=pl.CostEstimate(
            flops=5 * 2 * rows * rows * pairs * PAIR,
            bytes_accessed=rows * pairs * PAIR * 24,
            transcendentals=rows * rows * pairs * 2,
        ),
        name="attention_backward",
    )(low, live, start, queries, keys, values, grad, turned, log_total)


def row_major(values):
    return with_layout_constraint(values, Layout(major_to_minor=tuple(range(values.ndim))))


def cut_rows(values):
    *rest, rows, columns = values.shape
    block = next((b for b in (200, 192) if rows % b == 0), rows)
    return values.reshape(*rest, rows // block, block, columns)


def moved(values, axis, pairs):
    return row_major(lax.ppermute(row_major(cut_rows(values)), axis, pairs)).reshape(values.shape)


def across(values, axis, step):
    size = lax.axis_size(axis)
    return moved(values, axis, [(i, i ^ step) for i in range(size)])


def tied(values, *others):
    return lax.optimization_barrier((values, *others))[0]


def place(buffer, piece, index):
    return lax.dynamic_update_slice(buffer, piece[None], (index,) + (0,) * piece.ndim)


def leave_kernel(o_ref):
    pass


def unfilled(shape, dtype):
    return pl.pallas_call(
        leave_kernel,
        out_specs=pl.BlockSpec(memory_space=pl.ANY),
        out_shape=jax.ShapeDtypeStruct(shape, dtype),
        name="unfilled",
    )()


def ring(own, axis):
    size = lax.axis_size(axis)
    held, out = own, []
    for _ in range(size - 1):
        held = moved(held, axis, [(i, (i + 1) % size) for i in range(size)])
        out.append(held)
    return out


def gather_halves(shard, parts):
    size, here = lax.axis_size("fsdp"), lax.axis_index("fsdp")
    side = lax.axis_index("ctx")
    rows, columns = shard.shape
    width = columns // parts
    halves = shard.reshape(2, rows // 2, columns)
    own = lax.dynamic_index_in_dim(halves, side, 0, False)
    if size > 4:
        mine = lax.all_gather(own, "fsdp", axis=0)
        theirs = across(mine, "ctx", 1)
        both = jnp.where(side == 0, jnp.stack([mine, theirs], 1), jnp.stack([theirs, mine], 1))
        both = both.reshape(size * rows, columns)
        return [both[:, i * width : (i + 1) * width] for i in range(parts)], [mine] * (size - 1)
    whole = [
        lax.dynamic_update_slice(
            unfilled((2 * size, rows // 2, width), shard.dtype),
            halves[:, :, i * width : (i + 1) * width],
            (2 * here, 0, 0),
        )
        for i in range(parts)
    ]
    pieces = ring(own, "fsdp")
    for back, piece in enumerate(pieces, 1):
        other = across(piece, "ctx", 1)
        at = 2 * ((here + size - back) % size)
        for i in range(parts):
            span = slice(i * width, (i + 1) * width)
            whole[i] = place(whole[i], piece[:, span], at + side)
            whole[i] = place(whole[i], other[:, span], at + 1 - side)
    return [part.reshape(size * rows, width) for part in whole], pieces


def gather_direct(values):
    size, here = lax.axis_size("fsdp"), lax.axis_index("fsdp")
    if size > 4:
        return lax.all_gather(values, "fsdp", axis=0)
    whole = place(jnp.zeros((size, *values.shape), values.dtype), values, here)
    for back in range(1, size):
        piece = lax.ppermute(values, "fsdp", [(i, (i + back) % size) for i in range(size)])
        whole = place(whole, piece, (here + size - back) % size)
    return whole


def gather_whole(shard, after=()):
    size, here = lax.axis_size("fsdp"), lax.axis_index("fsdp")
    rows, columns = shard.shape
    own = tied(shard, *after)
    if size > 4:
        return lax.all_gather(own, "fsdp", axis=0, tiled=True), [own] * (size - 1)
    whole = place(unfilled((size, rows, columns), shard.dtype), own, here)
    pieces = ring(own, "fsdp")
    for back, piece in enumerate(pieces, 1):
        whole = place(whole, piece, (here + size - back) % size)
    return whole.reshape(size * rows, columns), pieces


def gather_pair(own, after=()):
    mine = row_major(lax.all_gather(tied(own, *after), "fsdp", axis=0, tiled=True))
    theirs = across(mine, "ctx", 1)
    return mine, theirs


def from_tp(own):
    beside = across(own, "tp", 2)
    return [own, across(own, "tp", 1), beside, across(beside, "tp", 1)]


FOLD = (0, 2, 1, 3)


def scatter_tp(terms):
    rows = terms[0][0].shape[0]

    def product(span):
        return sum(dot_lanes(left[span], right) for left, right in terms)

    gone = across(row_major(product(slice(rows // 2, rows)).astype(bf16)), "tp", 1)
    keep = row_major(product(slice(0, rows // 2)))
    far = keep[rows // 4 :] + gone[rows // 4 :].astype(f32)
    come = across(far.astype(bf16), "tp", 2)
    return keep[: rows // 4] + gone[: rows // 4].astype(f32) + come.astype(f32)


def by_xor(entries, index):
    odd, far = index % 2 == 1, index // 2 == 1
    a = [jnp.where(odd, entries[j ^ 1], entries[j]) for j in range(4)]
    return [jnp.where(far, a[j ^ 2], a[j]) for j in range(4)]


def assemble_kernel(index_ref, a_ref, b_ref, c_ref, d_ref, o_ref):
    j = pl.program_id(0) ^ index_ref[0]
    for step, piece in enumerate((a_ref, b_ref, c_ref, d_ref)):

        @pl.when(j == step)
        def _():
            o_ref[...] = piece[...].astype(o_ref.dtype)


def natural(entries, index, dtype):
    rows, columns = entries[0].shape
    return pl.pallas_call(
        assemble_kernel,
        grid=(len(entries),),
        in_specs=[pl.BlockSpec(memory_space=pltpu.SMEM)]
        + [pl.BlockSpec((rows, columns), lambda j: (0, 0))] * len(entries),
        out_specs=pl.BlockSpec((rows, columns), lambda j: (j, 0)),
        out_shape=jax.ShapeDtypeStruct((len(entries) * rows, columns), dtype),
        cost_estimate=pl.CostEstimate(
            flops=0, bytes_accessed=4 * len(entries) * rows * columns, transcendentals=0
        ),
        name="assemble",
    )(index.reshape(1), *entries)


def picked(stacked, index):
    return jnp.concatenate(
        [lax.dynamic_index_in_dim(stacked, index ^ j, 0, False) for j in FOLD], 0
    )


def spread_fsdp(both):
    return row_major(lax.psum_scatter(row_major(both), "fsdp", scatter_dimension=0, tiled=True))


def ring_sum(parts):
    size, here = lax.axis_size("fsdp"), lax.axis_index("fsdp")
    if size > 4:
        return lax.psum_scatter(parts, "fsdp", scatter_dimension=1)
    own = lambda back: lax.dynamic_index_in_dim(parts, (here + size - back) % size, 1, False)
    held = own(1)
    for back in range(2, size + 1):
        come = moved(held.astype(bf16), "fsdp", [(i, (i + 1) % size) for i in range(size)])
        held = come.astype(f32) + own(back % size).astype(f32)
    return held.astype(bf16)


def finish_rows(terms):
    size = lax.axis_size("fsdp")
    count, rows, columns = terms.shape
    mine = ring_sum(terms.reshape(count, size, rows // size, columns))
    return (mine.astype(f32) + across(mine, "ctx", 1).astype(f32)).astype(bf16)


def join_kernel(step, index_ref, *refs):
    o_ref = refs[-1]
    pieces = refs[:-1]
    count = pieces[0].shape[0]
    me = index_ref[0]
    out = []
    for part in range(count):
        for s in range(len(pieces)):
            value = pieces[0][part].astype(f32)
            for j in range(1, len(pieces)):
                value = jnp.where(me ^ s == j, pieces[j][part].astype(f32), value)
            out.append(value if s == len(pieces) - 1 else value[:, :step])
    o_ref[...] = jnp.concatenate(out, 1)


def join_windows(pieces, index, step):
    count, rows, reach = pieces[0].shape
    width = count * (step * (len(pieces) - 1) + reach)
    tall = rows // 5 if rows % 40 == 0 else rows
    return pl.pallas_call(
        partial(join_kernel, step),
        grid=(rows // tall,),
        in_specs=[pl.BlockSpec(memory_space=pltpu.SMEM)]
        + [pl.BlockSpec((count, tall, reach), lambda r: (0, r, 0))] * len(pieces),
        out_specs=pl.BlockSpec((tall, width), lambda r: (r, 0)),
        out_shape=jax.ShapeDtypeStruct((rows, width), f32),
        cost_estimate=pl.CostEstimate(flops=0, bytes_accessed=6 * rows * width, transcendentals=0),
        name="join_windows",
    )(index.reshape(1), *pieces)


def scatter_vectors(vectors, extra):
    size, here = lax.axis_size("fsdp"), lax.axis_index("fsdp")
    total = jnp.concatenate([vectors, extra[None]], 0)
    total = total + across(total, "ctx", 1)
    vectors, extra = total[:-1], total[-1:]
    vectors = vectors + across(vectors, "tp", 1)
    vectors = vectors + across(vectors, "tp", 2)
    total = jnp.concatenate([vectors, extra], 0)
    if size > 4:
        return lax.psum_scatter(total, "fsdp", scatter_dimension=1, tiled=True)
    count, width = total.shape
    parts = total.reshape(count, size, width // size).transpose(1, 0, 2)
    out = lax.dynamic_index_in_dim(parts, here, 0, False)
    for back in range(1, size):
        piece = lax.dynamic_index_in_dim(parts, (here + back) % size, 0, False)
        out = out + lax.ppermute(piece, "fsdp", [(i, (i + back) % size) for i in range(size)])
    return out


def on_device(
    tokens,
    segments,
    first_gain,
    first_bias,
    input_weight,
    query_bias,
    value_bias,
    output_weight,
    output_bias,
    second_gain,
    second_bias,
    up_weight,
    up_bias,
    down_weight,
    down_bias,
    cotangent,
):
    rows, width = tokens.shape
    members, me = lax.axis_size("tp"), lax.axis_index("tp")
    side = lax.axis_index("ctx")
    few = rows // members
    step = HEADS // members * HEAD
    reach = width - step * (members - 1)
    window = -(-reach // PAIR) * PAIR
    margin = window - reach

    def window_in(part):
        return jnp.pad(
            lax.dynamic_slice_in_dim(input_weight, part * width + me * step, reach, 1), ((0, 0), (0, margin))
        )

    hidden = up_weight.shape[1]
    cut = hidden // 2 // 128 * 128
    half = hidden - cut
    once = jnp.arange(half) < cut

    def halves(low, high):
        low = jnp.where(once.reshape((-1,) if low.ndim == 1 else (1, -1)), low, 0).astype(low.dtype)
        return jnp.where(side == 0, low, high), jnp.where(side == 0, high, low)

    def whole_of(mine, theirs):
        low, high = jnp.where(side == 0, mine, theirs), jnp.where(side == 0, theirs, mine)
        return jnp.concatenate([low[..., :cut], high], -1)

    windows_in = jnp.concatenate([window_in(part) for part in range(3)], 1)
    (weight_q, weight_k, weight_v), pieces_in = gather_halves(windows_in, 3)
    weight_out, _ = gather_whole(
        lax.dynamic_slice_in_dim(output_weight, me * step, reach, 1), (pieces_in[1],)
    )
    up_mine, up_theirs = gather_pair(halves(up_weight[:, :half], up_weight[:, cut:])[0], (pieces_in[0],))
    down_mine, down_theirs = gather_pair(halves(down_weight[:half].T, down_weight[cut:].T)[0], (pieces_in[0],))
    windows_out = from_tp(weight_out)

    small = [first_gain, first_bias, query_bias, value_bias, output_bias, second_gain, second_bias, up_bias, down_bias]
    small = jnp.stack(tied(small, windows_in))
    small = gather_direct(small).transpose(1, 0, 2).reshape(small.shape[0], width)
    gain_one, bias_one, bias_query, bias_value, bias_out, gain_two, bias_two, bias_up, bias_down = small.astype(f32)
    bias_mine, bias_theirs = halves(bias_up[:half], bias_up[cut:])

    def window_of(vector):
        return lax.dynamic_slice_in_dim(jnp.pad(vector, (0, margin)), me * step, window, 0)

    segments = tied(segments, pieces_in[0])
    labels = lax.dynamic_slice_in_dim(segments, side * rows, rows)
    start = jnp.sum((segments[:, None] < labels[None, :]).astype(jnp.int32), 0) + rows * (1 - side)
    low = start[::BLOCK] // BLOCK
    live = (me == members - 1).astype(jnp.int32).reshape(1)
    start = start.reshape(1, rows)

    earlier = lax.ppermute(tokens, "ctx", [(0, 1)])
    normed_one, normed_early = (
        norm_forward(part.astype(f32), gain_one, bias_one)[0].astype(bf16) for part in (tokens, earlier)
    )
    normed_all = jnp.concatenate([normed_early, normed_one], 0)
    keys = dot(normed_all, weight_k).astype(bf16)
    values = (dot(normed_all, weight_v) + window_of(bias_value)).astype(bf16)
    queries = (dot(normed_one, weight_q) + window_of(bias_query)).astype(bf16)
    upstream = picked(tied(cotangent, pieces_in[1]).reshape(members, few, width), me)
    queries, upstream = lax.optimization_barrier((queries, upstream))
    mixed, turned, log_total = attention_forward(low, live, start, queries, keys, values)

    def to_tp(pieces):
        come = [pieces[0]] + [across(pieces[j], "tp", j) for j in range(1, members)]
        return by_xor(come, me)

    blocks = mixed[:, :reach].reshape(members, few, reach)
    come = to_tp([lax.dynamic_index_in_dim(blocks, me ^ j, 0, False) for j in range(members)])
    mixture = jnp.concatenate([come[j][:, :step] for j in range(members - 1)] + [come[members - 1]], 1)

    own_tokens = lax.dynamic_slice_in_dim(tokens, me * few, few).astype(f32)
    branch = by_xor([dot(mixture, part) for part in windows_out], me)
    branch = jnp.concatenate([branch[j][:, :step] for j in range(members - 1)] + [branch[members - 1]], 1)
    middle = own_tokens + branch + bias_out
    normed, unit_two, inverse_two = norm_forward(middle, gain_two, bias_two)
    normed_two = from_tp(normed.astype(bf16))
    normed_two = jnp.concatenate([normed_two[j] for j in FOLD], 0)

    def hidden_half(weight_up, weight_down, bias):
        grad_activated = dot(upstream, weight_down)
        preact = dot(normed_two, weight_up) + bias
        activated, gelu_pull = jax.vjp(gelu_tanh, preact)
        return activated.astype(bf16), gelu_pull(grad_activated)[0].astype(bf16)

    act_mine, pre_mine = hidden_half(up_mine, down_mine, bias_mine)
    act_theirs, pre_theirs = hidden_half(up_theirs, down_theirs, bias_theirs)
    grad_normed = scatter_tp([(pre_mine, up_mine), (pre_theirs, up_theirs)])
    down_gone = dot_rows(upstream, act_theirs).astype(bf16)
    up_gone = dot_rows(normed_two, pre_theirs).astype(bf16)
    up_kept = dot_rows(normed_two, pre_mine).astype(bf16)
    grad_normed = tied(grad_normed, down_gone, up_gone, up_kept)
    own_upstream = upstream[:few].astype(f32)
    grad_two, grad_gain_two, grad_bias_two = norm_backward(grad_normed, unit_two, inverse_two, gain_two)
    grad_middle = own_upstream + grad_two
    grad_branch = grad_middle.astype(bf16)

    inner = jnp.arange(reach) < step

    def columns_for(index):
        return lax.dynamic_slice_in_dim(grad_branch, index * step, reach, 1)

    branch_windows = [columns_for(me ^ j) for j in range(members)]
    grad_mixture = jnp.zeros((few, width), f32)
    for j in range(members):
        once = jnp.where(inner | ((me ^ j) == members - 1), branch_windows[j], 0).astype(bf16)
        grad_mixture += dot_lanes(once, windows_out[j])
    grad_mixture = jnp.pad(grad_mixture.astype(bf16), ((0, 0), (0, margin)))
    come = to_tp([lax.dynamic_slice_in_dim(grad_mixture, (me ^ j) * step, window, 1) for j in range(members)])
    grad_mixed = jnp.concatenate(come, 0)

    up_gone, up_kept = spread_fsdp(up_gone), spread_fsdp(up_kept)
    other_gone, other_kept = across(up_gone, "ctx", 1), across(up_kept, "ctx", 1)
    down_kept = dot_rows(upstream, act_mine) + across(down_gone, "ctx", 1).astype(f32)
    down_kept = down_kept.astype(bf16)
    down_sum = spread_fsdp(down_kept)
    shard_down = whole_of(down_sum, across(down_sum, "ctx", 1)).astype(f32).T
    shard_up = whole_of(
        up_kept.astype(f32) + other_gone.astype(f32),
        up_gone.astype(f32) + other_kept.astype(f32),
    )
    late_mine, late_theirs = tied((act_mine, act_theirs), grad_mixture)
    result = scatter_tp([(late_mine, down_mine), (late_theirs, down_theirs)])
    result = (middle + result + bias_down).astype(bf16)
    result = natural(from_tp(result), me, bf16)

    def branch_product(j):
        return dot_rows(mixture, branch_windows[j])

    come = across(jnp.stack([branch_product(1), branch_product(3)]).astype(bf16), "tp", 1).astype(f32)
    near = branch_product(0) + come[0]
    far = (branch_product(2) + come[1]).astype(bf16)
    near = (near + across(far, "tp", 2).astype(f32)).astype(bf16)
    shard_out = join_windows(from_tp(finish_rows(near[None])), me, step)

    grad_mixed = tied(grad_mixed, down_kept)
    grad_q, grad_k, grad_v = attention_backward(
        low, live, start, queries, keys, values, grad_mixed, turned, log_total
    )
    grad_in = jnp.stack(
        [
            row_major(dot_rows(left, grad[:, :reach]).astype(bf16).reshape(4, -1, reach)).reshape(width, reach)
            for left, grad in ((normed_one, grad_q), (normed_all, grad_k), (normed_all, grad_v))
        ]
    )
    shard_in = join_windows(from_tp(finish_rows(grad_in)), me, step)

    def turned_rows(grad):
        return picked(grad.reshape(members, few, window), me)

    grad_early = scatter_tp(
        [(turned_rows(grad[:rows]), weight) for grad, weight in ((grad_k, weight_k), (grad_v, weight_v))]
    )
    grad_normed = scatter_tp(
        [
            (turned_rows(grad), weight)
            for grad, weight in ((grad_q, weight_q), (grad_k[rows:], weight_k), (grad_v[rows:], weight_v))
        ]
    )
    grad_normed += moved(grad_early.astype(bf16), "ctx", [(1, 0)]).astype(f32)
    _, unit_one, inverse_one = norm_forward(own_tokens, gain_one, bias_one)
    grad_one, grad_gain_one, grad_bias_one = norm_backward(grad_normed, unit_one, inverse_one, gain_one)
    gradient = (grad_middle + grad_one).astype(bf16)
    gradient = natural(from_tp(gradient), me, bf16)

    def spread(columns):
        wide = jnp.zeros((width + margin,), f32)
        columns = jnp.where(jnp.arange(window) < jnp.where(me == members - 1, reach, step), columns, 0.0)
        return lax.dynamic_update_slice_in_dim(wide, columns, me * step, 0)[:width]

    vectors = jnp.stack(
        [
            grad_gain_one,
            grad_bias_one,
            spread(jnp.sum(grad_q.astype(f32), 0)),
            spread(jnp.sum(grad_v.astype(f32), 0)),
            jnp.sum(grad_branch.astype(f32), 0),
            grad_gain_two,
            grad_bias_two,
            jnp.sum(own_upstream, 0),
        ]
    )
    grad_bias_up = whole_of(jnp.sum(pre_mine.astype(f32), 0), jnp.sum(pre_theirs.astype(f32), 0))
    vectors = scatter_vectors(vectors, grad_bias_up)
    return (
        result,
        gradient,
        vectors[0],
        vectors[1],
        shard_in,
        vectors[2],
        vectors[3],
        shard_out,
        vectors[4],
        vectors[5],
        vectors[6],
        shard_up,
        vectors[8],
        shard_down,
        vectors[7],
    )


def solution(mesh):
    return jax.shard_map(
        on_device,
        mesh=mesh,
        in_specs=(
            P(("fsdp", "ctx"), None),
            P("fsdp"),
            P("fsdp"),
            P("fsdp"),
            P("fsdp", None),
            P("fsdp"),
            P("fsdp"),
            P("fsdp", None),
            P("fsdp"),
            P("fsdp"),
            P("fsdp"),
            P("fsdp", "tp"),
            P(("tp", "fsdp")),
            P("tp", "fsdp"),
            P("fsdp"),
            P(("fsdp", "ctx"), None),
        ),
        out_specs=(
            P(("fsdp", "ctx"), None),
            P(("fsdp", "ctx"), None),
            P("fsdp"),
            P("fsdp"),
            P("fsdp", None),
            P("fsdp"),
            P("fsdp"),
            P("fsdp", None),
            P("fsdp"),
            P("fsdp"),
            P("fsdp"),
            P("fsdp", "tp"),
            P(("tp", "fsdp")),
            P("tp", "fsdp"),
            P("fsdp"),
        ),
        check_vma=False,
    )
```

```python
from functools import partial

import jax
import jax.numpy as jnp
from jax import lax
from jax.experimental import pallas as pl
from jax.experimental.layout import Layout, with_layout_constraint
from jax.experimental.pallas import tpu as pltpu
from jax.sharding import PartitionSpec as P


HEADS = 25
HEAD = 64
PAIR = 2 * HEAD
BLOCK = 256

EPS = 1e-05
NEGATIVE = -1e30
SCALE = HEAD ** (-0.5)

bf16 = jnp.bfloat16
f32 = jnp.float32


def norm_forward(values, gain, offset):
    centre = values - jnp.mean(values, -1, keepdims=True)
    inverse = lax.rsqrt(jnp.mean(centre * centre, -1, keepdims=True) + EPS)
    unit = centre * inverse
    return (unit * gain + offset, unit, inverse)


def norm_backward(upstream, unit, inverse, gain):
    scaled = upstream * gain
    inner = (
        scaled
        - jnp.mean(scaled, -1, keepdims=True)
        - unit * jnp.mean(scaled * unit, -1, keepdims=True)
    )
    return (inner * inverse, jnp.sum(upstream * unit, 0), jnp.sum(upstream, 0))


def gelu_tanh(values):
    return jax.nn.gelu(values, approximate=True)


def dot_rows(left, right):
    return lax.dot_general(left, right, (((0,), (0,)), ((), ())), preferred_element_type=f32)


def dot_lanes(left, right):
    return lax.dot_general(left, right, (((1,), (1,)), ((), ())), preferred_element_type=f32)


def dot(left, right):
    return jnp.dot(left, right, preferred_element_type=f32)


def lane_mask(which):
    lanes = lax.broadcasted_iota(jnp.int32, (1, PAIR), 1)
    return (lanes // HEAD == which).astype(f32)


def masked_pair(block, scale):
    wide = block.astype(f32)
    return [(wide * (lane_mask(h) * scale)).astype(bf16) for h in range(2)]


def allowed_block(key_block, query_block, rows, start):
    keys = key_block * BLOCK + lax.broadcasted_iota(jnp.int32, (BLOCK, BLOCK), 0)
    places = (
        rows + query_block * BLOCK + lax.broadcasted_iota(jnp.int32, (BLOCK, BLOCK), 1)
    )
    return (keys >= start) & (keys <= places)


def forward_kernel(
    low_ref, live_ref, start_ref, q_ref, k_ref, v_ref, o_ref, ot_ref, log_ref, vtbuf
):
    rows = q_ref.shape[0]
    pair = pl.program_id(0)
    live = (pair < pl.num_programs(0) - 1) | (live_ref[0] > 0)

    @pl.when(jnp.logical_not(live))
    def _():
        o_ref[...] = jnp.zeros_like(o_ref)
        ot_ref[...] = jnp.zeros_like(ot_ref)
        log_ref[...] = jnp.zeros_like(log_ref)

    @pl.when(live)
    def _():
        vtbuf[...] = v_ref[...].astype(f32).T.astype(bf16)
        for qb in range(rows // BLOCK):
            span = slice(qb * BLOCK, (qb + 1) * BLOCK)
            queries = masked_pair(q_ref[span, :], SCALE)
            start = start_ref[:, span]

            def step(kb, carry):
                base = pl.multiple_of(kb * BLOCK, BLOCK)
                keys = k_ref[pl.ds(base, BLOCK), :]
                allowed = allowed_block(kb, qb, rows, start)
                out = []
                for h in range(2):
                    highest, summed, total = carry[3 * h : 3 * h + 3]
                    scores = jnp.where(allowed, dot_lanes(keys, queries[h]), NEGATIVE)
                    higher = jnp.maximum(highest, jnp.max(scores, 0, keepdims=True))
                    fade = jnp.exp(highest - higher)
                    expo = jnp.exp(scores - higher)
                    summed = summed * fade + jnp.sum(expo, 0, keepdims=True)
                    values = vtbuf[h * HEAD : (h + 1) * HEAD, pl.ds(base, BLOCK)]
                    total = total * fade + dot(values, expo.astype(bf16))
                    out += [higher, summed, total]
                return tuple(out)

            empty = (
                jnp.full((1, BLOCK), NEGATIVE, f32),
                jnp.zeros((1, BLOCK), f32),
                jnp.zeros((HEAD, BLOCK), f32),
            )
            done = lax.fori_loop(low_ref[qb], rows // BLOCK + qb + 1, step, empty + empty)
            for h in range(2):
                highest, summed, total = done[3 * h : 3 * h + 3]
                ot_ref[h * HEAD : (h + 1) * HEAD, span] = total / summed
                log_ref[0, h : h + 1, span] = highest + jnp.log(summed)
            o_ref[span, :] = ot_ref[:, span].T.astype(bf16)


def backward_kernel(
    low_ref,
    live_ref,
    start_ref,
    q_ref,
    k_ref,
    v_ref,
    g_ref,
    ot_ref,
    log_ref,
    o_ref,
    ktbuf,
    dkbuf,
    dvbuf,
):
    rows = q_ref.shape[0]
    pair, part = pl.program_id(0), pl.program_id(1)
    live = (pair < pl.num_programs(0) - 1) | (live_ref[0] > 0)

    @pl.when(part == 0)
    def _():
        dkbuf[...] = jnp.zeros_like(dkbuf)
        dvbuf[...] = jnp.zeros_like(dvbuf)
        o_ref[:rows, :] = jnp.zeros((rows, PAIR), bf16)

    @pl.when((part == 0) & jnp.logical_not(live))
    def _():
        o_ref[rows:, :] = jnp.zeros((rows, PAIR), bf16)

    @pl.when((part == 0) & live)
    def _():
        ktbuf[...] = k_ref[...].astype(f32).T.astype(bf16)
        for qb in range(rows // BLOCK):
            span = slice(qb * BLOCK, (qb + 1) * BLOCK)
            queries = masked_pair(q_ref[span, :], SCALE)
            grads = masked_pair(g_ref[span, :], 1.0)
            start = start_ref[:, span]
            turned = g_ref[span, :].astype(f32).T * ot_ref[:, span]
            inner = [jnp.sum(turned[h * HEAD : (h + 1) * HEAD], 0, keepdims=True) for h in range(2)]
            log_total = [log_ref[0, h : h + 1, span] for h in range(2)]

            def step(kb, carry):
                base = pl.multiple_of(kb * BLOCK, BLOCK)
                here = pl.ds(base, BLOCK)
                keys, values = k_ref[here, :], v_ref[here, :]
                allowed = allowed_block(kb, qb, rows, start)
                out = []
                grad_keys, grad_values = dkbuf[here, :], dvbuf[here, :]
                for h in range(2):
                    scores = jnp.where(allowed, dot_lanes(keys, queries[h]), NEGATIVE)
                    probs = jnp.exp(scores - log_total[h])
                    grad_probs = dot_lanes(values, grads[h])
                    grad_scores = (probs * (grad_probs - inner[h])).astype(bf16)
                    grad_values += dot(probs.astype(bf16), grads[h])
                    grad_keys += dot(grad_scores, queries[h])
                    turned_keys = ktbuf[h * HEAD : (h + 1) * HEAD, here]
                    out.append(carry[h] + dot(turned_keys, grad_scores))
                dkbuf[here, :] = grad_keys
                dvbuf[here, :] = grad_values
                return tuple(out)

            empty = jnp.zeros((HEAD, BLOCK), f32)
            done = lax.fori_loop(low_ref[qb], rows // BLOCK + qb + 1, step, (empty, empty))
            into = slice(rows + qb * BLOCK, rows + (qb + 1) * BLOCK)
            o_ref[into, :] = (jnp.concatenate(done, 0) * SCALE).T.astype(bf16)

    @pl.when(part == 1)
    def _():
        o_ref[...] = dkbuf[...].astype(bf16)

    @pl.when(part == 2)
    def _():
        o_ref[...] = dvbuf[...].astype(bf16)


def attention_specs(rows, pairs):
    smem = pl.BlockSpec(memory_space=pltpu.SMEM)
    return [
        smem,
        smem,
        pl.BlockSpec((1, rows), lambda p, *_: (0, 0)),
        pl.BlockSpec((rows, PAIR), lambda p, *_: (1, p)),
        pl.BlockSpec((2 * rows, PAIR), lambda p, *_: (0, pairs + p)),
        pl.BlockSpec((2 * rows, PAIR), lambda p, *_: (0, 2 * pairs + p)),
    ]


def attention_forward(low, live, start, joined):
    rows, pairs = joined.shape[0] // 2, joined.shape[1] // (3 * PAIR)
    return pl.pallas_call(
        forward_kernel,
        grid=(pairs,),
        in_specs=attention_specs(rows, pairs),
        out_specs=[
            pl.BlockSpec((rows, PAIR), lambda p: (0, p)),
            pl.BlockSpec((PAIR, rows), lambda p: (p, 0)),
            pl.BlockSpec((1, 2, rows), lambda p: (p, 0, 0)),
        ],
        out_shape=[
            jax.ShapeDtypeStruct((rows, pairs * PAIR), bf16),
            jax.ShapeDtypeStruct((pairs * PAIR, rows), f32),
            jax.ShapeDtypeStruct((pairs, 2, rows), f32),
        ],
        scratch_shapes=[pltpu.VMEM((PAIR, 2 * rows), bf16)],
        cost_estimate=pl.CostEstimate(
            flops=2 * 2 * rows * rows * pairs * PAIR,
            bytes_accessed=rows * pairs * PAIR * 16,
            transcendentals=rows * rows * pairs * 2,
        ),
        name="attention_forward",
    )(low, live, start, joined, joined, joined)


def attention_backward(low, live, start, joined, grad, turned, log_total):
    rows, pairs = joined.shape[0] // 2, joined.shape[1] // (3 * PAIR)
    return pl.pallas_call(
        backward_kernel,
        grid=(pairs, 3),
        in_specs=attention_specs(rows, pairs)
        + [
            pl.BlockSpec((rows, PAIR), lambda p, *_: (0, p)),
            pl.BlockSpec((PAIR, rows), lambda p, *_: (p, 0)),
            pl.BlockSpec((1, 2, rows), lambda p, *_: (p, 0, 0)),
        ],
        out_specs=pl.BlockSpec((2 * rows, PAIR), lambda p, part: (0, part * pairs + p)),
        out_shape=jax.ShapeDtypeStruct(joined.shape, bf16),
        scratch_shapes=[
            pltpu.VMEM((PAIR, 2 * rows), bf16),
            pltpu.VMEM((2 * rows, PAIR), f32),
            pltpu.VMEM((2 * rows, PAIR), f32),
        ],
        cost_estimate=pl.CostEstimate(
            flops=5 * 2 * rows * rows * pairs * PAIR,
            bytes_accessed=rows * pairs * PAIR * 24,
            transcendentals=rows * rows * pairs * 2,
        ),
        name="attention_backward",
    )(low, live, start, joined, joined, joined, grad, turned, log_total)


def row_major(values):
    return with_layout_constraint(values, Layout(major_to_minor=tuple(range(values.ndim))))


def cut_rows(values):
    *rest, rows, columns = values.shape
    block = next((b for b in (200, 192) if rows % b == 0), rows)
    return values.reshape(*rest, rows // block, block, columns)


def moved(values, axis, pairs):
    return row_major(lax.ppermute(row_major(cut_rows(values)), axis, pairs)).reshape(values.shape)


def across(values, axis, step):
    size = lax.axis_size(axis)
    return moved(values, axis, [(i, i ^ step) for i in range(size)])


def tied(values, *others):
    return lax.optimization_barrier((values, *others))[0]


def place(buffer, piece, index):
    return lax.dynamic_update_slice(buffer, piece[None], (index,) + (0,) * piece.ndim)


def leave_kernel(o_ref):
    pass


def unfilled(shape, dtype):
    return pl.pallas_call(
        leave_kernel,
        out_specs=pl.BlockSpec(memory_space=pl.ANY),
        out_shape=jax.ShapeDtypeStruct(shape, dtype),
        name="unfilled",
    )()


def ring(own, axis):
    size = lax.axis_size(axis)
    held, out = own, []
    for _ in range(size - 1):
        held = moved(held, axis, [(i, (i + 1) % size) for i in range(size)])
        out.append(held)
    return out


def gather_halves(shard):
    size, here = lax.axis_size("fsdp"), lax.axis_index("fsdp")
    side = lax.axis_index("ctx")
    rows, columns = shard.shape
    halves = shard.reshape(2, rows // 2, columns)
    own = lax.dynamic_index_in_dim(halves, side, 0, False)
    if size > 4:
        mine = lax.all_gather(own, "fsdp", axis=0)
        theirs = across(mine, "ctx", 1)
        both = jnp.where(side == 0, jnp.stack([mine, theirs], 1), jnp.stack([theirs, mine], 1))
        return both.reshape(size * rows, columns), [mine] * (size - 1)
    whole = unfilled((2 * size, rows // 2, columns), shard.dtype)
    whole = lax.dynamic_update_slice(whole, halves, (2 * here, 0, 0))
    pieces = ring(own, "fsdp")
    for back, piece in enumerate(pieces, 1):
        other = across(piece, "ctx", 1)
        at = 2 * ((here + size - back) % size)
        whole = place(whole, piece, at + side)
        whole = place(whole, other, at + 1 - side)
    return whole.reshape(size * rows, columns), pieces


def gather_direct(values):
    size, here = lax.axis_size("fsdp"), lax.axis_index("fsdp")
    if size > 4:
        return lax.all_gather(values, "fsdp", axis=0)
    whole = place(jnp.zeros((size, *values.shape), values.dtype), values, here)
    for back in range(1, size):
        piece = lax.ppermute(values, "fsdp", [(i, (i + back) % size) for i in range(size)])
        whole = place(whole, piece, (here + size - back) % size)
    return whole


def gather_whole(shard, after=()):
    size, here = lax.axis_size("fsdp"), lax.axis_index("fsdp")
    rows, columns = shard.shape
    own = tied(shard, *after)
    if size > 4:
        return lax.all_gather(own, "fsdp", axis=0, tiled=True)
    whole = place(unfilled((size, rows, columns), shard.dtype), own, here)
    for back in range(1, size):
        piece = moved(own, "fsdp", [(i, (i + back) % size) for i in range(size)])
        whole = place(whole, piece, (here + size - back) % size)
    return whole.reshape(size * rows, columns)


def gather_pair(own, after=()):
    mine = row_major(lax.all_gather(tied(own, *after), "fsdp", axis=0, tiled=True))
    theirs = across(mine, "ctx", 1)
    return mine, theirs


def from_tp(own, after=()):
    beside = tied(across(own, "tp", 2), *after)
    return [own, across(own, "tp", 1), beside, across(beside, "tp", 1)]


FOLD = (0, 2, 1, 3)


def scatter_tp(terms):
    rows = terms[0][0].shape[0]

    def product(span):
        return sum(dot_lanes(left[span], right) for left, right in terms)

    gone = across(row_major(product(slice(rows // 2, rows)).astype(bf16)), "tp", 1)
    keep = row_major(product(slice(0, rows // 2)))
    far = keep[rows // 4 :] + gone[rows // 4 :].astype(f32)
    come = across(far.astype(bf16), "tp", 2)
    return keep[: rows // 4] + gone[: rows // 4].astype(f32) + come.astype(f32)


def by_xor(entries, index):
    odd, far = index % 2 == 1, index // 2 == 1
    a = [jnp.where(odd, entries[j ^ 1], entries[j]) for j in range(4)]
    return [jnp.where(far, a[j ^ 2], a[j]) for j in range(4)]


def assemble_kernel(index_ref, a_ref, b_ref, c_ref, d_ref, o_ref):
    j = pl.program_id(0) ^ index_ref[0]
    for step, piece in enumerate((a_ref, b_ref, c_ref, d_ref)):

        @pl.when(j == step)
        def _():
            o_ref[...] = piece[...].astype(o_ref.dtype)


def natural(entries, index, dtype):
    rows, columns = entries[0].shape
    return pl.pallas_call(
        assemble_kernel,
        grid=(len(entries),),
        in_specs=[pl.BlockSpec(memory_space=pltpu.SMEM)]
        + [pl.BlockSpec((rows, columns), lambda j: (0, 0))] * len(entries),
        out_specs=pl.BlockSpec((rows, columns), lambda j: (j, 0)),
        out_shape=jax.ShapeDtypeStruct((len(entries) * rows, columns), dtype),
        cost_estimate=pl.CostEstimate(
            flops=0, bytes_accessed=4 * len(entries) * rows * columns, transcendentals=0
        ),
        name="assemble",
    )(index.reshape(1), *entries)


def picked(stacked, index):
    return jnp.concatenate(
        [lax.dynamic_index_in_dim(stacked, index ^ j, 0, False) for j in FOLD], 0
    )


def spread_fsdp(both):
    return row_major(lax.psum_scatter(row_major(both), "fsdp", scatter_dimension=0, tiled=True))


def finish_rows(terms, chunks):
    mine = spread_fsdp(terms)
    chunks = chunks if mine.shape[0] % (8 * chunks) == 0 else 1
    rows, out = mine.shape[0] // chunks, []
    for i in range(chunks):
        piece = mine[i * rows : (i + 1) * rows]
        out.append(from_tp((piece.astype(f32) + across(piece, "ctx", 1).astype(f32)).astype(bf16)))
    return out


def join_kernel(step, reach, index_ref, *refs):
    o_ref = refs[-1]
    members = 4
    chunks = (len(refs) - 1) // members
    width = refs[0].shape[1]
    me = index_ref[0]
    count = -(-width // (reach + PAIR))
    window = width // count
    for chunk in range(chunks):
        pieces = refs[chunk * members : (chunk + 1) * members]

        @pl.when(pl.program_id(0) // (pl.num_programs(0) // chunks) == chunk)
        def _():
            out = []
            for s in range(members):
                value = pieces[0][...].astype(f32)
                for j in range(1, members):
                    value = jnp.where(me ^ s == j, pieces[j][...].astype(f32), value)
                out.append(value)
            o_ref[...] = jnp.concatenate(
                [
                    out[s][:, part * window : part * window + (reach if s == members - 1 else step)]
                    for part in range(count)
                    for s in range(members)
                ],
                1,
            )


def join_windows(chunks, index, step, reach):
    rows, width = chunks[0][0].shape
    members = len(chunks[0])
    whole = -(-width // (reach + PAIR)) * (step * (members - 1) + reach)
    steps = next((n for n in (5, 1) if rows % (8 * n) == 0), 1)
    tall = rows // steps

    def spec(chunk):
        return pl.BlockSpec((tall, width), lambda r: (jnp.clip(r - chunk * steps, 0, steps - 1), 0))

    return pl.pallas_call(
        partial(join_kernel, step, reach),
        grid=(len(chunks) * steps,),
        in_specs=[pl.BlockSpec(memory_space=pltpu.SMEM)] + [spec(i) for i in range(len(chunks)) for _ in range(members)],
        out_specs=pl.BlockSpec((tall, whole), lambda r: (r, 0)),
        out_shape=jax.ShapeDtypeStruct((len(chunks) * rows, whole), f32),
        cost_estimate=pl.CostEstimate(flops=0, bytes_accessed=6 * rows * whole, transcendentals=0),
        name="join_windows",
    )(index.reshape(1), *[piece for chunk in chunks for piece in chunk])


def scatter_vectors(vectors, extra):
    size, here = lax.axis_size("fsdp"), lax.axis_index("fsdp")
    total = jnp.concatenate([vectors, extra[None]], 0)
    total = total + across(total, "ctx", 1)
    vectors, extra = total[:-1], total[-1:]
    vectors = vectors + across(vectors, "tp", 1)
    vectors = vectors + across(vectors, "tp", 2)
    total = jnp.concatenate([vectors, extra], 0)
    if size > 4:
        return lax.psum_scatter(total, "fsdp", scatter_dimension=1, tiled=True)
    count, width = total.shape
    parts = total.reshape(count, size, width // size).transpose(1, 0, 2)
    out = lax.dynamic_index_in_dim(parts, here, 0, False)
    for back in range(1, size):
        piece = lax.dynamic_index_in_dim(parts, (here + back) % size, 0, False)
        out = out + lax.ppermute(piece, "fsdp", [(i, (i + back) % size) for i in range(size)])
    return out


def on_device(
    tokens,
    segments,
    first_gain,
    first_bias,
    input_weight,
    query_bias,
    value_bias,
    output_weight,
    output_bias,
    second_gain,
    second_bias,
    up_weight,
    up_bias,
    down_weight,
    down_bias,
    cotangent,
):
    rows, width = tokens.shape
    members, me = lax.axis_size("tp"), lax.axis_index("tp")
    side = lax.axis_index("ctx")
    few = rows // members
    step = HEADS // members * HEAD
    reach = width - step * (members - 1)
    window = -(-reach // PAIR) * PAIR
    margin = window - reach

    def window_in(part):
        return jnp.pad(
            lax.dynamic_slice_in_dim(input_weight, part * width + me * step, reach, 1), ((0, 0), (0, margin))
        )

    hidden = up_weight.shape[1]
    cut = hidden // 2 // 128 * 128
    half = hidden - cut
    once = jnp.arange(half) < cut

    def halves(low, high):
        low = jnp.where(once.reshape((-1,) if low.ndim == 1 else (1, -1)), low, 0).astype(low.dtype)
        return jnp.where(side == 0, low, high), jnp.where(side == 0, high, low)

    def whole_of(mine, theirs):
        low, high = jnp.where(side == 0, mine, theirs), jnp.where(side == 0, theirs, mine)
        return jnp.concatenate([low[..., :cut], high], -1)

    windows_in = jnp.concatenate([window_in(part) for part in range(3)], 1)
    weight_in, pieces_in = gather_halves(windows_in)
    weight_out = gather_whole(lax.dynamic_slice_in_dim(output_weight, me * step, reach, 1), (pieces_in[1],))
    up_mine, up_theirs = gather_pair(halves(up_weight[:, :half], up_weight[:, cut:])[0], (pieces_in[0],))
    downs = jnp.stack(halves(down_weight[:half].T, down_weight[cut:].T))
    downs = row_major(lax.all_gather(tied(downs, pieces_in[0]), "fsdp", axis=0))
    down_mine, down_theirs = (downs[:, i].reshape(width, half) for i in range(2))

    small = [first_gain, first_bias, query_bias, value_bias, output_bias, second_gain, second_bias, up_bias, down_bias]
    small = jnp.stack(tied(small, windows_in))
    small = gather_direct(small).transpose(1, 0, 2).reshape(small.shape[0], width)
    gain_one, bias_one, bias_query, bias_value, bias_out, gain_two, bias_two, bias_up, bias_down = small.astype(f32)
    bias_mine, bias_theirs = halves(bias_up[:half], bias_up[cut:])

    def window_of(vector):
        return lax.dynamic_slice_in_dim(jnp.pad(vector, (0, margin)), me * step, window, 0)

    segments = tied(segments, pieces_in[0])
    labels = lax.dynamic_slice_in_dim(segments, side * rows, rows)
    start = jnp.sum((segments[:, None] < labels[None, :]).astype(jnp.int32), 0) + rows * (1 - side)
    low = start[::BLOCK] // BLOCK
    live = (me == members - 1).astype(jnp.int32).reshape(1)
    start = start.reshape(1, rows)

    earlier = lax.ppermute(tokens, "ctx", [(0, 1)])
    normed_one, normed_early = (
        norm_forward(part.astype(f32), gain_one, bias_one)[0].astype(bf16) for part in (tokens, earlier)
    )
    normed_all = jnp.concatenate([normed_early, normed_one], 0)
    bias_in = jnp.concatenate([window_of(bias_query), jnp.zeros((window,), f32), window_of(bias_value)])
    joined = (dot(normed_all, weight_in) + bias_in).astype(bf16)
    upstream = picked(tied(cotangent, pieces_in[1]).reshape(members, few, width), me)
    joined, upstream = lax.optimization_barrier((joined, upstream))
    mixed, turned, log_total = attention_forward(low, live, start, joined)

    windows_out = from_tp(weight_out, (mixed,))

    def to_tp(pieces):
        come = [pieces[0]] + [across(pieces[j], "tp", j) for j in range(1, members)]
        return by_xor(come, me)

    blocks = mixed[:, :reach].reshape(members, few, reach)
    come = to_tp([lax.dynamic_index_in_dim(blocks, me ^ j, 0, False) for j in range(members)])
    mixture = jnp.concatenate([come[j][:, :step] for j in range(members - 1)] + [come[members - 1]], 1)

    own_tokens = lax.dynamic_slice_in_dim(tokens, me * few, few).astype(f32)
    branch = by_xor([dot(mixture, part) for part in windows_out], me)
    branch = jnp.concatenate([branch[j][:, :step] for j in range(members - 1)] + [branch[members - 1]], 1)
    middle = own_tokens + branch + bias_out
    normed, unit_two, inverse_two = norm_forward(middle, gain_two, bias_two)
    normed_two = from_tp(normed.astype(bf16))
    normed_two = jnp.concatenate([normed_two[j] for j in FOLD], 0)

    def hidden_half(normed, weight_up, weight_down, bias):
        grad_activated = dot(upstream, weight_down)
        preact = dot(normed, weight_up) + bias
        activated, gelu_pull = jax.vjp(gelu_tanh, preact)
        return activated.astype(bf16), gelu_pull(grad_activated)[0].astype(bf16)

    act_theirs, pre_theirs = hidden_half(normed_two, up_theirs, down_theirs, bias_theirs)
    down_gone = row_major(cut_rows(dot_rows(upstream, act_theirs).astype(bf16)))
    down_come = across(down_gone, "ctx", 1)
    act_mine, pre_mine = hidden_half(tied(normed_two, down_gone), up_mine, down_mine, bias_mine)
    grad_normed = scatter_tp([(pre_mine, up_mine), (pre_theirs, up_theirs)])
    up_gone = dot_rows(normed_two, pre_theirs).astype(bf16)
    up_kept = dot_rows(normed_two, pre_mine).astype(bf16)
    grad_normed = tied(grad_normed, up_gone, up_kept)
    own_upstream = upstream[:few].astype(f32)
    grad_two, grad_gain_two, grad_bias_two = norm_backward(grad_normed, unit_two, inverse_two, gain_two)
    grad_middle = own_upstream + grad_two
    grad_branch = grad_middle.astype(bf16)

    inner = jnp.arange(reach) < step

    def columns_for(index):
        return lax.dynamic_slice_in_dim(grad_branch, index * step, reach, 1)

    branch_windows = [columns_for(me ^ j) for j in range(members)]
    grad_mixture = jnp.zeros((few, width), f32)
    for j in range(members):
        once = jnp.where(inner | ((me ^ j) == members - 1), branch_windows[j], 0).astype(bf16)
        grad_mixture += dot_lanes(once, windows_out[j])
    grad_mixture = jnp.pad(grad_mixture.astype(bf16), ((0, 0), (0, margin)))
    come = to_tp([lax.dynamic_slice_in_dim(grad_mixture, (me ^ j) * step, window, 1) for j in range(members)])
    grad_mixed = jnp.concatenate(come, 0)

    up_gone, up_kept = spread_fsdp(up_gone), spread_fsdp(up_kept)
    other_gone, other_kept = across(up_gone, "ctx", 1), across(up_kept, "ctx", 1)
    late_mine = tied(act_mine, grad_mixture)
    down_kept = row_major(cut_rows(dot_rows(upstream, late_mine))) + down_come.astype(f32)
    down_kept = down_kept.astype(bf16).reshape(width, half)
    down_sum = spread_fsdp(down_kept)
    shard_down = whole_of(down_sum, across(down_sum, "ctx", 1)).astype(f32).T
    shard_up = whole_of(
        up_kept.astype(f32) + other_gone.astype(f32),
        up_gone.astype(f32) + other_kept.astype(f32),
    )
    late_mine, late_theirs = tied((act_mine, act_theirs), grad_mixture)
    result = scatter_tp([(late_mine, down_mine), (late_theirs, down_theirs)])
    result = from_tp((middle + result + bias_down).astype(bf16))

    grad_mixed = tied(grad_mixed, down_kept)
    grads = attention_backward(low, live, start, joined, grad_mixed, turned, log_total)
    grad_in = row_major(dot_rows(normed_all, grads).astype(bf16))
    shard_in = join_windows(finish_rows(grad_in, 2), me, step, reach)

    late_mixture, late_windows = tied((mixture, branch_windows), grads)

    def branch_product(j):
        return row_major(cut_rows(dot_rows(late_mixture, late_windows[j])))

    come = [across(branch_product(j).astype(bf16), "tp", 1).astype(f32) for j in (1, 3)]
    near = branch_product(0) + come[0]
    far = (branch_product(2) + come[1]).astype(bf16)
    come = across(far, "tp", 2)
    near = (near + come.astype(f32)).astype(bf16).reshape(width, reach)
    shard_out = join_windows(finish_rows(tied(near, grad_in), 1), me, step, reach)
    result = natural(tied(result, grads), me, bf16)

    both = jnp.stack([grads[rows:].reshape(members, few, -1), grads[:rows].reshape(members, few, -1)], 1)
    both = picked(tied(both, far).reshape(members, 2 * few, -1), me)
    grad_normed = scatter_tp([(both, weight_in)])
    grad_early = moved(grad_normed[few:].astype(bf16), "ctx", [(1, 0)])
    grad_normed = grad_normed[:few] + grad_early.astype(f32)
    _, unit_one, inverse_one = norm_forward(own_tokens, gain_one, bias_one)
    grad_one, grad_gain_one, grad_bias_one = norm_backward(grad_normed, unit_one, inverse_one, gain_one)
    gradient = (grad_middle + grad_one).astype(bf16)
    gradient = natural(from_tp(gradient), me, bf16)

    def spread(columns):
        wide = jnp.zeros((width + margin,), f32)
        columns = jnp.where(jnp.arange(window) < jnp.where(me == members - 1, reach, step), columns, 0.0)
        return lax.dynamic_update_slice_in_dim(wide, columns, me * step, 0)[:width]

    grad_sums = jnp.sum(grads.astype(f32), 0)
    vectors = jnp.stack(
        [
            grad_gain_one,
            grad_bias_one,
            spread(grad_sums[:window]),
            spread(grad_sums[2 * window :]),
            jnp.sum(grad_branch.astype(f32), 0),
            grad_gain_two,
            grad_bias_two,
            jnp.sum(own_upstream, 0),
        ]
    )
    grad_bias_up = whole_of(jnp.sum(pre_mine.astype(f32), 0), jnp.sum(pre_theirs.astype(f32), 0))
    vectors = scatter_vectors(vectors, grad_bias_up)
    return (
        result,
        gradient,
        vectors[0],
        vectors[1],
        shard_in,
        vectors[2],
        vectors[3],
        shard_out,
        vectors[4],
        vectors[5],
        vectors[6],
        shard_up,
        vectors[8],
        shard_down,
        vectors[7],
    )


def solution(mesh):
    return jax.shard_map(
        on_device,
        mesh=mesh,
        in_specs=(
            P(("fsdp", "ctx"), None),
            P("fsdp"),
            P("fsdp"),
            P("fsdp"),
            P("fsdp", None),
            P("fsdp"),
            P("fsdp"),
            P("fsdp", None),
            P("fsdp"),
            P("fsdp"),
            P("fsdp"),
            P("fsdp", "tp"),
            P(("tp", "fsdp")),
            P("tp", "fsdp"),
            P("fsdp"),
            P(("fsdp", "ctx"), None),
        ),
        out_specs=(
            P(("fsdp", "ctx"), None),
            P(("fsdp", "ctx"), None),
            P("fsdp"),
            P("fsdp"),
            P("fsdp", None),
            P("fsdp"),
            P("fsdp"),
            P("fsdp", None),
            P("fsdp"),
            P("fsdp"),
            P("fsdp"),
            P("fsdp", "tp"),
            P(("tp", "fsdp")),
            P("tp", "fsdp"),
            P("fsdp"),
        ),
        check_vma=False,
    )
```

```python
from functools import partial

import jax
import jax.numpy as jnp
from jax import lax
from jax.experimental import pallas as pl
from jax.experimental.layout import Layout, with_layout_constraint
from jax.experimental.pallas import tpu as pltpu
from jax.sharding import PartitionSpec as P


HEADS = 25
HEAD = 64
PAIR = 2 * HEAD
BLOCK = 256

EPS = 1e-05
NEGATIVE = -1e30
SCALE = HEAD ** (-0.5)

bf16 = jnp.bfloat16
f32 = jnp.float32


def norm_forward(values, gain, offset):
    centre = values - jnp.mean(values, -1, keepdims=True)
    inverse = lax.rsqrt(jnp.mean(centre * centre, -1, keepdims=True) + EPS)
    unit = centre * inverse
    return (unit * gain + offset, unit, inverse)


def norm_backward(upstream, unit, inverse, gain):
    scaled = upstream * gain
    inner = (
        scaled
        - jnp.mean(scaled, -1, keepdims=True)
        - unit * jnp.mean(scaled * unit, -1, keepdims=True)
    )
    return (inner * inverse, jnp.sum(upstream * unit, 0), jnp.sum(upstream, 0))


def gelu_tanh(values):
    return jax.nn.gelu(values, approximate=True)


def dot_rows(left, right):
    return lax.dot_general(left, right, (((0,), (0,)), ((), ())), preferred_element_type=f32)


def dot_lanes(left, right):
    return lax.dot_general(left, right, (((1,), (1,)), ((), ())), preferred_element_type=f32)


def dot(left, right):
    return jnp.dot(left, right, preferred_element_type=f32)


def lane_mask(which):
    lanes = lax.broadcasted_iota(jnp.int32, (1, PAIR), 1)
    return (lanes // HEAD == which).astype(f32)


def masked_pair(block, scale):
    wide = block.astype(f32)
    return [(wide * (lane_mask(h) * scale)).astype(bf16) for h in range(2)]


def allowed_block(key_block, query_block, rows, start):
    keys = key_block * BLOCK + lax.broadcasted_iota(jnp.int32, (BLOCK, BLOCK), 0)
    places = (
        rows + query_block * BLOCK + lax.broadcasted_iota(jnp.int32, (BLOCK, BLOCK), 1)
    )
    return (keys >= start) & (keys <= places)


def forward_kernel(
    low_ref, live_ref, start_ref, q_ref, k_ref, v_ref, o_ref, ot_ref, log_ref, vtbuf
):
    rows = q_ref.shape[0]
    pair = pl.program_id(0)
    live = (pair < pl.num_programs(0) - 1) | (live_ref[0] > 0)

    @pl.when(jnp.logical_not(live))
    def _():
        o_ref[...] = jnp.zeros_like(o_ref)
        ot_ref[...] = jnp.zeros_like(ot_ref)
        log_ref[...] = jnp.zeros_like(log_ref)

    @pl.when(live)
    def _():
        vtbuf[...] = v_ref[...].astype(f32).T.astype(bf16)
        for qb in range(rows // BLOCK):
            span = slice(qb * BLOCK, (qb + 1) * BLOCK)
            queries = masked_pair(q_ref[span, :], SCALE)
            start = start_ref[:, span]

            def step(kb, carry):
                base = pl.multiple_of(kb * BLOCK, BLOCK)
                keys = k_ref[pl.ds(base, BLOCK), :]
                allowed = allowed_block(kb, qb, rows, start)
                out = []
                for h in range(2):
                    highest, summed, total = carry[3 * h : 3 * h + 3]
                    scores = jnp.where(allowed, dot_lanes(keys, queries[h]), NEGATIVE)
                    higher = jnp.maximum(highest, jnp.max(scores, 0, keepdims=True))
                    fade = jnp.exp(highest - higher)
                    expo = jnp.exp(scores - higher)
                    summed = summed * fade + jnp.sum(expo, 0, keepdims=True)
                    values = vtbuf[h * HEAD : (h + 1) * HEAD, pl.ds(base, BLOCK)]
                    total = total * fade + dot(values, expo.astype(bf16))
                    out += [higher, summed, total]
                return tuple(out)

            empty = (
                jnp.full((1, BLOCK), NEGATIVE, f32),
                jnp.zeros((1, BLOCK), f32),
                jnp.zeros((HEAD, BLOCK), f32),
            )
            done = lax.fori_loop(low_ref[qb], rows // BLOCK + qb + 1, step, empty + empty)
            for h in range(2):
                highest, summed, total = done[3 * h : 3 * h + 3]
                ot_ref[h * HEAD : (h + 1) * HEAD, span] = total / summed
                log_ref[0, h : h + 1, span] = highest + jnp.log(summed)
            o_ref[span, :] = ot_ref[:, span].T.astype(bf16)


def backward_kernel(
    low_ref,
    live_ref,
    start_ref,
    q_ref,
    k_ref,
    v_ref,
    g_ref,
    ot_ref,
    log_ref,
    o_ref,
    ktbuf,
    dkbuf,
    dvbuf,
):
    rows = q_ref.shape[0]
    pair, part = pl.program_id(0), pl.program_id(1)
    live = (pair < pl.num_programs(0) - 1) | (live_ref[0] > 0)

    @pl.when(part == 0)
    def _():
        dkbuf[...] = jnp.zeros_like(dkbuf)
        dvbuf[...] = jnp.zeros_like(dvbuf)
        o_ref[:rows, :] = jnp.zeros((rows, PAIR), bf16)

    @pl.when((part == 0) & jnp.logical_not(live))
    def _():
        o_ref[rows:, :] = jnp.zeros((rows, PAIR), bf16)

    @pl.when((part == 0) & live)
    def _():
        ktbuf[...] = k_ref[...].astype(f32).T.astype(bf16)
        for qb in range(rows // BLOCK):
            span = slice(qb * BLOCK, (qb + 1) * BLOCK)
            queries = masked_pair(q_ref[span, :], SCALE)
            grads = masked_pair(g_ref[span, :], 1.0)
            start = start_ref[:, span]
            turned = g_ref[span, :].astype(f32).T * ot_ref[:, span]
            inner = [jnp.sum(turned[h * HEAD : (h + 1) * HEAD], 0, keepdims=True) for h in range(2)]
            log_total = [log_ref[0, h : h + 1, span] for h in range(2)]

            def step(kb, carry):
                base = pl.multiple_of(kb * BLOCK, BLOCK)
                here = pl.ds(base, BLOCK)
                keys, values = k_ref[here, :], v_ref[here, :]
                allowed = allowed_block(kb, qb, rows, start)
                out = []
                grad_keys, grad_values = dkbuf[here, :], dvbuf[here, :]
                for h in range(2):
                    scores = jnp.where(allowed, dot_lanes(keys, queries[h]), NEGATIVE)
                    probs = jnp.exp(scores - log_total[h])
                    grad_probs = dot_lanes(values, grads[h])
                    grad_scores = (probs * (grad_probs - inner[h])).astype(bf16)
                    grad_values += dot(probs.astype(bf16), grads[h])
                    grad_keys += dot(grad_scores, queries[h])
                    turned_keys = ktbuf[h * HEAD : (h + 1) * HEAD, here]
                    out.append(carry[h] + dot(turned_keys, grad_scores))
                dkbuf[here, :] = grad_keys
                dvbuf[here, :] = grad_values
                return tuple(out)

            empty = jnp.zeros((HEAD, BLOCK), f32)
            done = lax.fori_loop(low_ref[qb], rows // BLOCK + qb + 1, step, (empty, empty))
            into = slice(rows + qb * BLOCK, rows + (qb + 1) * BLOCK)
            o_ref[into, :] = (jnp.concatenate(done, 0) * SCALE).T.astype(bf16)

    @pl.when(part == 1)
    def _():
        o_ref[...] = dkbuf[...].astype(bf16)

    @pl.when(part == 2)
    def _():
        o_ref[...] = dvbuf[...].astype(bf16)


def attention_specs(rows, pairs):
    smem = pl.BlockSpec(memory_space=pltpu.SMEM)
    return [
        smem,
        smem,
        pl.BlockSpec((1, rows), lambda p, *_: (0, 0)),
        pl.BlockSpec((rows, PAIR), lambda p, *_: (1, p)),
        pl.BlockSpec((2 * rows, PAIR), lambda p, *_: (0, pairs + p)),
        pl.BlockSpec((2 * rows, PAIR), lambda p, *_: (0, 2 * pairs + p)),
    ]


def attention_forward(low, live, start, joined):
    rows, pairs = joined.shape[0] // 2, joined.shape[1] // (3 * PAIR)
    return pl.pallas_call(
        forward_kernel,
        grid=(pairs,),
        in_specs=attention_specs(rows, pairs),
        out_specs=[
            pl.BlockSpec((rows, PAIR), lambda p: (0, p)),
            pl.BlockSpec((PAIR, rows), lambda p: (p, 0)),
            pl.BlockSpec((1, 2, rows), lambda p: (p, 0, 0)),
        ],
        out_shape=[
            jax.ShapeDtypeStruct((rows, pairs * PAIR), bf16),
            jax.ShapeDtypeStruct((pairs * PAIR, rows), f32),
            jax.ShapeDtypeStruct((pairs, 2, rows), f32),
        ],
        scratch_shapes=[pltpu.VMEM((PAIR, 2 * rows), bf16)],
        cost_estimate=pl.CostEstimate(
            flops=2 * 2 * rows * rows * pairs * PAIR,
            bytes_accessed=rows * pairs * PAIR * 16,
            transcendentals=rows * rows * pairs * 2,
        ),
        name="attention_forward",
    )(low, live, start, joined, joined, joined)


def attention_backward(low, live, start, joined, grad, turned, log_total):
    rows, pairs = joined.shape[0] // 2, joined.shape[1] // (3 * PAIR)
    return pl.pallas_call(
        backward_kernel,
        grid=(pairs, 3),
        in_specs=attention_specs(rows, pairs)
        + [
            pl.BlockSpec((rows, PAIR), lambda p, *_: (0, p)),
            pl.BlockSpec((PAIR, rows), lambda p, *_: (p, 0)),
            pl.BlockSpec((1, 2, rows), lambda p, *_: (p, 0, 0)),
        ],
        out_specs=pl.BlockSpec((2 * rows, PAIR), lambda p, part: (0, part * pairs + p)),
        out_shape=jax.ShapeDtypeStruct(joined.shape, bf16),
        scratch_shapes=[
            pltpu.VMEM((PAIR, 2 * rows), bf16),
            pltpu.VMEM((2 * rows, PAIR), f32),
            pltpu.VMEM((2 * rows, PAIR), f32),
        ],
        cost_estimate=pl.CostEstimate(
            flops=5 * 2 * rows * rows * pairs * PAIR,
            bytes_accessed=rows * pairs * PAIR * 24,
            transcendentals=rows * rows * pairs * 2,
        ),
        name="attention_backward",
    )(low, live, start, joined, joined, joined, grad, turned, log_total)


def row_major(values):
    return with_layout_constraint(values, Layout(major_to_minor=tuple(range(values.ndim))))


def cut_rows(values):
    *rest, rows, columns = values.shape
    block = next((b for b in (200, 192) if rows % b == 0), rows)
    return values.reshape(*rest, rows // block, block, columns)


def moved(values, axis, pairs):
    return row_major(lax.ppermute(row_major(cut_rows(values)), axis, pairs)).reshape(values.shape)


def across(values, axis, step):
    size = lax.axis_size(axis)
    return moved(values, axis, [(i, i ^ step) for i in range(size)])


def tied(values, *others):
    return lax.optimization_barrier((values, *others))[0]


def place(buffer, piece, index):
    return lax.dynamic_update_slice(buffer, piece[None], (index,) + (0,) * piece.ndim)


def leave_kernel(o_ref):
    pass


def unfilled(shape, dtype):
    return pl.pallas_call(
        leave_kernel,
        out_specs=pl.BlockSpec(memory_space=pl.ANY),
        out_shape=jax.ShapeDtypeStruct(shape, dtype),
        name="unfilled",
    )()


def ring(own, axis):
    size = lax.axis_size(axis)
    held, out = own, []
    for _ in range(size - 1):
        held = moved(held, axis, [(i, (i + 1) % size) for i in range(size)])
        out.append(held)
    return out


def gather_halves(shard):
    size, here = lax.axis_size("fsdp"), lax.axis_index("fsdp")
    side = lax.axis_index("ctx")
    rows, columns = shard.shape
    halves = shard.reshape(2, rows // 2, columns)
    own = lax.dynamic_index_in_dim(halves, side, 0, False)
    if size > 4:
        mine = lax.all_gather(own, "fsdp", axis=0)
        theirs = across(mine, "ctx", 1)
        both = jnp.where(side == 0, jnp.stack([mine, theirs], 1), jnp.stack([theirs, mine], 1))
        return both.reshape(size * rows, columns), [mine] * (size - 1)
    whole = unfilled((2 * size, rows // 2, columns), shard.dtype)
    whole = lax.dynamic_update_slice(whole, halves, (2 * here, 0, 0))
    pieces = ring(own, "fsdp")
    for back, piece in enumerate(pieces, 1):
        other = across(piece, "ctx", 1)
        at = 2 * ((here + size - back) % size)
        whole = place(whole, piece, at + side)
        whole = place(whole, other, at + 1 - side)
    return whole.reshape(size * rows, columns), pieces


def gather_direct(values):
    size, here = lax.axis_size("fsdp"), lax.axis_index("fsdp")
    if size > 4:
        return lax.all_gather(values, "fsdp", axis=0)
    whole = place(jnp.zeros((size, *values.shape), values.dtype), values, here)
    for back in range(1, size):
        piece = lax.ppermute(values, "fsdp", [(i, (i + back) % size) for i in range(size)])
        whole = place(whole, piece, (here + size - back) % size)
    return whole


def gather_whole(shard, after=()):
    size, here = lax.axis_size("fsdp"), lax.axis_index("fsdp")
    rows, columns = shard.shape
    own = tied(shard, *after)
    if size > 4:
        return lax.all_gather(own, "fsdp", axis=0, tiled=True)
    whole = place(unfilled((size, rows, columns), shard.dtype), own, here)
    for back in range(1, size):
        piece = moved(own, "fsdp", [(i, (i + back) % size) for i in range(size)])
        whole = place(whole, piece, (here + size - back) % size)
    return whole.reshape(size * rows, columns)


def gather_pair(own, after=()):
    mine = row_major(lax.all_gather(tied(own, *after), "fsdp", axis=0, tiled=True))
    theirs = across(mine, "ctx", 1)
    return mine, theirs


def from_tp(own, after=()):
    beside = tied(across(own, "tp", 2), *after)
    return [own, across(own, "tp", 1), beside, across(beside, "tp", 1)]


FOLD = (0, 2, 1, 3)


def scatter_tp(terms):
    rows = terms[0][0].shape[0]

    def product(span):
        return sum(dot_lanes(left[span], right) for left, right in terms)

    gone = across(row_major(product(slice(rows // 2, rows)).astype(bf16)), "tp", 1)
    keep = row_major(product(slice(0, rows // 2)))
    far = keep[rows // 4 :] + gone[rows // 4 :].astype(f32)
    come = across(far.astype(bf16), "tp", 2)
    return keep[: rows // 4] + gone[: rows // 4].astype(f32) + come.astype(f32)


def by_xor(entries, index):
    odd, far = index % 2 == 1, index // 2 == 1
    a = [jnp.where(odd, entries[j ^ 1], entries[j]) for j in range(4)]
    return [jnp.where(far, a[j ^ 2], a[j]) for j in range(4)]


def assemble_kernel(index_ref, a_ref, b_ref, c_ref, d_ref, o_ref):
    j = pl.program_id(0) ^ index_ref[0]
    for step, piece in enumerate((a_ref, b_ref, c_ref, d_ref)):

        @pl.when(j == step)
        def _():
            o_ref[...] = piece[...].astype(o_ref.dtype)


def natural(entries, index, dtype):
    rows, columns = entries[0].shape
    return pl.pallas_call(
        assemble_kernel,
        grid=(len(entries),),
        in_specs=[pl.BlockSpec(memory_space=pltpu.SMEM)]
        + [pl.BlockSpec((rows, columns), lambda j: (0, 0))] * len(entries),
        out_specs=pl.BlockSpec((rows, columns), lambda j: (j, 0)),
        out_shape=jax.ShapeDtypeStruct((len(entries) * rows, columns), dtype),
        cost_estimate=pl.CostEstimate(
            flops=0, bytes_accessed=4 * len(entries) * rows * columns, transcendentals=0
        ),
        name="assemble",
    )(index.reshape(1), *entries)


def picked(stacked, index):
    return jnp.concatenate(
        [lax.dynamic_index_in_dim(stacked, index ^ j, 0, False) for j in FOLD], 0
    )


def spread_fsdp(both):
    return row_major(lax.psum_scatter(row_major(both), "fsdp", scatter_dimension=0, tiled=True))


def finish_rows(terms, chunks, after=()):
    mine = tied(spread_fsdp(terms), *after)
    chunks = chunks if mine.shape[0] % (8 * chunks) == 0 else 1
    rows, out = mine.shape[0] // chunks, []
    for i in range(chunks):
        piece = mine[i * rows : (i + 1) * rows]
        out.append(from_tp((piece.astype(f32) + across(piece, "ctx", 1).astype(f32)).astype(bf16)))
    return out


def join_kernel(step, reach, index_ref, *refs):
    o_ref = refs[-1]
    members = 4
    chunks = (len(refs) - 1) // members
    width = refs[0].shape[1]
    me = index_ref[0]
    count = -(-width // (reach + PAIR))
    window = width // count
    for chunk in range(chunks):
        pieces = refs[chunk * members : (chunk + 1) * members]

        @pl.when(pl.program_id(0) // (pl.num_programs(0) // chunks) == chunk)
        def _():
            out = []
            for s in range(members):
                value = pieces[0][...].astype(f32)
                for j in range(1, members):
                    value = jnp.where(me ^ s == j, pieces[j][...].astype(f32), value)
                out.append(value)
            o_ref[...] = jnp.concatenate(
                [
                    out[s][:, part * window : part * window + (reach if s == members - 1 else step)]
                    for part in range(count)
                    for s in range(members)
                ],
                1,
            )


def join_windows(chunks, index, step, reach):
    rows, width = chunks[0][0].shape
    members = len(chunks[0])
    whole = -(-width // (reach + PAIR)) * (step * (members - 1) + reach)
    steps = next((n for n in (5, 1) if rows % (8 * n) == 0), 1)
    tall = rows // steps

    def spec(chunk):
        return pl.BlockSpec((tall, width), lambda r: (jnp.clip(r - chunk * steps, 0, steps - 1), 0))

    return pl.pallas_call(
        partial(join_kernel, step, reach),
        grid=(len(chunks) * steps,),
        in_specs=[pl.BlockSpec(memory_space=pltpu.SMEM)] + [spec(i) for i in range(len(chunks)) for _ in range(members)],
        out_specs=pl.BlockSpec((tall, whole), lambda r: (r, 0)),
        out_shape=jax.ShapeDtypeStruct((len(chunks) * rows, whole), f32),
        cost_estimate=pl.CostEstimate(flops=0, bytes_accessed=6 * rows * whole, transcendentals=0),
        name="join_windows",
    )(index.reshape(1), *[piece for chunk in chunks for piece in chunk])


def scatter_vectors(vectors, extra):
    size, here = lax.axis_size("fsdp"), lax.axis_index("fsdp")
    total = jnp.concatenate([vectors, extra[None]], 0)
    total = total + across(total, "ctx", 1)
    vectors, extra = total[:-1], total[-1:]
    vectors = vectors + across(vectors, "tp", 1)
    vectors = vectors + across(vectors, "tp", 2)
    total = jnp.concatenate([vectors, extra], 0)
    if size > 4:
        return lax.psum_scatter(total, "fsdp", scatter_dimension=1, tiled=True)
    count, width = total.shape
    parts = total.reshape(count, size, width // size).transpose(1, 0, 2)
    out = lax.dynamic_index_in_dim(parts, here, 0, False)
    for back in range(1, size):
        piece = lax.dynamic_index_in_dim(parts, (here + back) % size, 0, False)
        out = out + lax.ppermute(piece, "fsdp", [(i, (i + back) % size) for i in range(size)])
    return out


def on_device(
    tokens,
    segments,
    first_gain,
    first_bias,
    input_weight,
    query_bias,
    value_bias,
    output_weight,
    output_bias,
    second_gain,
    second_bias,
    up_weight,
    up_bias,
    down_weight,
    down_bias,
    cotangent,
):
    rows, width = tokens.shape
    members, me = lax.axis_size("tp"), lax.axis_index("tp")
    side = lax.axis_index("ctx")
    few = rows // members
    step = HEADS // members * HEAD
    reach = width - step * (members - 1)
    window = -(-reach // PAIR) * PAIR
    margin = window - reach

    def window_in(part):
        return jnp.pad(
            lax.dynamic_slice_in_dim(input_weight, part * width + me * step, reach, 1), ((0, 0), (0, margin))
        )

    hidden = up_weight.shape[1]
    cut = hidden // 2 // 128 * 128
    half = hidden - cut
    once = jnp.arange(half) < cut

    def halves(low, high):
        low = jnp.where(once.reshape((-1,) if low.ndim == 1 else (1, -1)), low, 0).astype(low.dtype)
        return jnp.where(side == 0, low, high), jnp.where(side == 0, high, low)

    def whole_of(mine, theirs):
        low, high = jnp.where(side == 0, mine, theirs), jnp.where(side == 0, theirs, mine)
        return jnp.concatenate([low[..., :cut], high], -1)

    windows_in = jnp.concatenate([window_in(part) for part in range(3)], 1)
    weight_in, pieces_in = gather_halves(windows_in)
    weight_out = gather_whole(lax.dynamic_slice_in_dim(output_weight, me * step, reach, 1), (pieces_in[1],))
    up_mine, up_theirs = gather_pair(halves(up_weight[:, :half], up_weight[:, cut:])[0], (pieces_in[0],))
    downs = jnp.stack(halves(down_weight[:half].T, down_weight[cut:].T))
    downs = row_major(lax.all_gather(tied(downs, pieces_in[0]), "fsdp", axis=0))
    down_mine, down_theirs = (downs[:, i].reshape(width, half) for i in range(2))

    small = [first_gain, first_bias, query_bias, value_bias, output_bias, second_gain, second_bias, up_bias, down_bias]
    small = jnp.stack(tied(small, windows_in))
    small = gather_direct(small).transpose(1, 0, 2).reshape(small.shape[0], width)
    gain_one, bias_one, bias_query, bias_value, bias_out, gain_two, bias_two, bias_up, bias_down = small.astype(f32)
    bias_mine, bias_theirs = halves(bias_up[:half], bias_up[cut:])

    def window_of(vector):
        return lax.dynamic_slice_in_dim(jnp.pad(vector, (0, margin)), me * step, window, 0)

    segments = tied(segments, pieces_in[0])
    labels = lax.dynamic_slice_in_dim(segments, side * rows, rows)
    start = jnp.sum((segments[:, None] < labels[None, :]).astype(jnp.int32), 0) + rows * (1 - side)
    low = start[::BLOCK] // BLOCK
    live = (me == members - 1).astype(jnp.int32).reshape(1)
    start = start.reshape(1, rows)

    earlier = lax.ppermute(tokens, "ctx", [(0, 1)])
    normed_one, normed_early = (
        norm_forward(part.astype(f32), gain_one, bias_one)[0].astype(bf16) for part in (tokens, earlier)
    )
    normed_all = jnp.concatenate([normed_early, normed_one], 0)
    bias_in = jnp.concatenate([window_of(bias_query), jnp.zeros((window,), f32), window_of(bias_value)])
    joined = (dot(normed_all, weight_in) + bias_in).astype(bf16)
    upstream = picked(tied(cotangent, pieces_in[1]).reshape(members, few, width), me)
    joined, upstream = lax.optimization_barrier((joined, upstream))
    mixed, turned, log_total = attention_forward(low, live, start, joined)

    windows_out = from_tp(weight_out, (mixed,))

    def to_tp(pieces):
        come = [pieces[0]] + [across(pieces[j], "tp", j) for j in range(1, members)]
        return by_xor(come, me)

    blocks = mixed[:, :reach].reshape(members, few, reach)
    come = to_tp([lax.dynamic_index_in_dim(blocks, me ^ j, 0, False) for j in range(members)])
    mixture = jnp.concatenate([come[j][:, :step] for j in range(members - 1)] + [come[members - 1]], 1)

    own_tokens = lax.dynamic_slice_in_dim(tokens, me * few, few).astype(f32)
    branch = by_xor([dot(mixture, part) for part in windows_out], me)
    branch = jnp.concatenate([branch[j][:, :step] for j in range(members - 1)] + [branch[members - 1]], 1)
    middle = own_tokens + branch + bias_out
    normed, unit_two, inverse_two = norm_forward(middle, gain_two, bias_two)
    normed_two = from_tp(normed.astype(bf16))
    normed_two = jnp.concatenate([normed_two[j] for j in FOLD], 0)

    def hidden_half(normed, weight_up, weight_down, bias):
        grad_activated = dot(upstream, weight_down)
        preact = dot(normed, weight_up) + bias
        activated, gelu_pull = jax.vjp(gelu_tanh, preact)
        return activated.astype(bf16), gelu_pull(grad_activated)[0].astype(bf16)

    act_theirs, pre_theirs = hidden_half(normed_two, up_theirs, down_theirs, bias_theirs)
    down_gone = row_major(cut_rows(dot_rows(upstream, act_theirs).astype(bf16)))
    down_come = across(down_gone, "ctx", 1)
    act_mine, pre_mine = hidden_half(tied(normed_two, down_gone), up_mine, down_mine, bias_mine)
    grad_normed = scatter_tp([(pre_mine, up_mine), (pre_theirs, up_theirs)])
    up_gone = dot_rows(normed_two, pre_theirs).astype(bf16)
    up_kept = dot_rows(normed_two, pre_mine).astype(bf16)
    grad_normed = tied(grad_normed, up_gone, up_kept)
    own_upstream = upstream[:few].astype(f32)
    grad_two, grad_gain_two, grad_bias_two = norm_backward(grad_normed, unit_two, inverse_two, gain_two)
    grad_middle = own_upstream + grad_two
    grad_branch = grad_middle.astype(bf16)

    inner = jnp.arange(reach) < step

    def columns_for(index):
        return lax.dynamic_slice_in_dim(grad_branch, index * step, reach, 1)

    branch_windows = [columns_for(me ^ j) for j in range(members)]
    grad_mixture = jnp.zeros((few, width), f32)
    for j in range(members):
        once = jnp.where(inner | ((me ^ j) == members - 1), branch_windows[j], 0).astype(bf16)
        grad_mixture += dot_lanes(once, windows_out[j])
    grad_mixture = jnp.pad(grad_mixture.astype(bf16), ((0, 0), (0, margin)))
    come = to_tp([lax.dynamic_slice_in_dim(grad_mixture, (me ^ j) * step, window, 1) for j in range(members)])
    grad_mixed = jnp.concatenate(come, 0)

    up_gone, up_kept = spread_fsdp(up_gone), spread_fsdp(up_kept)
    other_gone, other_kept = across(up_gone, "ctx", 1), across(up_kept, "ctx", 1)
    late_mine = tied(act_mine, grad_mixture)
    down_kept = row_major(cut_rows(dot_rows(upstream, late_mine))) + down_come.astype(f32)
    down_kept = down_kept.astype(bf16).reshape(width, half)
    down_sum = spread_fsdp(down_kept)
    shard_down = whole_of(down_sum, across(down_sum, "ctx", 1)).astype(f32).T
    shard_up = whole_of(
        up_kept.astype(f32) + other_gone.astype(f32),
        up_gone.astype(f32) + other_kept.astype(f32),
    )
    late_mine, late_theirs = tied((act_mine, act_theirs), grad_mixture)
    result = scatter_tp([(late_mine, down_mine), (late_theirs, down_theirs)])
    result = from_tp((middle + result + bias_down).astype(bf16))

    grad_mixed = tied(grad_mixed, down_kept)
    grads = attention_backward(low, live, start, joined, grad_mixed, turned, log_total)
    grad_in = row_major(dot_rows(normed_all, grads).astype(bf16))
    chunks_in = finish_rows(grad_in, 2)
    shard_in = join_windows(chunks_in, me, step, reach)

    late_mixture, late_windows = tied((mixture, branch_windows), grads)

    def branch_product(j):
        return row_major(cut_rows(dot_rows(late_mixture, late_windows[j])))

    come = [across(branch_product(j).astype(bf16), "tp", 1).astype(f32) for j in (1, 3)]
    near = branch_product(0) + come[0]
    far = (branch_product(2) + come[1]).astype(bf16)
    come = across(far, "tp", 2)
    near = (near + come.astype(f32)).astype(bf16).reshape(width, reach)
    shard_out = join_windows(
        finish_rows(tied(near, grad_in), 1, (chunks_in[-1][0],)), me, step, reach
    )
    result = natural(tied(result, grads), me, bf16)

    both = jnp.stack([grads[rows:].reshape(members, few, -1), grads[:rows].reshape(members, few, -1)], 1)
    both = picked(tied(both, far).reshape(members, 2 * few, -1), me)
    grad_normed = scatter_tp([(both, weight_in)])
    grad_early = moved(grad_normed[few:].astype(bf16), "ctx", [(1, 0)])
    grad_normed = grad_normed[:few] + grad_early.astype(f32)
    _, unit_one, inverse_one = norm_forward(own_tokens, gain_one, bias_one)
    grad_one, grad_gain_one, grad_bias_one = norm_backward(grad_normed, unit_one, inverse_one, gain_one)
    gradient = (grad_middle + grad_one).astype(bf16)
    gradient = natural(from_tp(gradient), me, bf16)

    def spread(columns):
        wide = jnp.zeros((width + margin,), f32)
        columns = jnp.where(jnp.arange(window) < jnp.where(me == members - 1, reach, step), columns, 0.0)
        return lax.dynamic_update_slice_in_dim(wide, columns, me * step, 0)[:width]

    grad_sums = jnp.sum(grads.astype(f32), 0)
    vectors = jnp.stack(
        [
            grad_gain_one,
            grad_bias_one,
            spread(grad_sums[:window]),
            spread(grad_sums[2 * window :]),
            jnp.sum(grad_branch.astype(f32), 0),
            grad_gain_two,
            grad_bias_two,
            jnp.sum(own_upstream, 0),
        ]
    )
    grad_bias_up = whole_of(jnp.sum(pre_mine.astype(f32), 0), jnp.sum(pre_theirs.astype(f32), 0))
    vectors = scatter_vectors(vectors, grad_bias_up)
    return (
        result,
        gradient,
        vectors[0],
        vectors[1],
        shard_in,
        vectors[2],
        vectors[3],
        shard_out,
        vectors[4],
        vectors[5],
        vectors[6],
        shard_up,
        vectors[8],
        shard_down,
        vectors[7],
    )


def solution(mesh):
    return jax.shard_map(
        on_device,
        mesh=mesh,
        in_specs=(
            P(("fsdp", "ctx"), None),
            P("fsdp"),
            P("fsdp"),
            P("fsdp"),
            P("fsdp", None),
            P("fsdp"),
            P("fsdp"),
            P("fsdp", None),
            P("fsdp"),
            P("fsdp"),
            P("fsdp"),
            P("fsdp", "tp"),
            P(("tp", "fsdp")),
            P("tp", "fsdp"),
            P("fsdp"),
            P(("fsdp", "ctx"), None),
        ),
        out_specs=(
            P(("fsdp", "ctx"), None),
            P(("fsdp", "ctx"), None),
            P("fsdp"),
            P("fsdp"),
            P("fsdp", None),
            P("fsdp"),
            P("fsdp"),
            P("fsdp", None),
            P("fsdp"),
            P("fsdp"),
            P("fsdp"),
            P("fsdp", "tp"),
            P(("tp", "fsdp")),
            P("tp", "fsdp"),
            P("fsdp"),
        ),
        check_vma=False,
    )
```
